512 devices in a mesh: grp: 16 (over z_hi, y), seq: 32 (over x, z_lo, core).
Axes of the slice: x: 4, y: 8, z: 8 (z_hi: 2, z_lo: 4; z = z_hi * 4 + z_lo), core: 2. Of those that a mesh axis runs over, the one named last changes fastest.
Arguments:
- tokens: bfloat16 [65536, 2048], P(('grp', 'seq')), may hold values from -6.6 to 6.6
- grad_output: bfloat16 [65536, 2048], P(('grp', 'seq')), may hold values from -6 to 6
- query_gain: float32 [2048], replicated, may hold values from -6 to 6
- key_gain: float32 [2048], replicated, may hold values from -6 to 6
- short_query_gain: float32 [2048], replicated, may hold values from -24 to 24
- short_key_gain: float32 [2048], replicated, may hold values from -24 to 24
Outputs:
- grad_tokens: bfloat16 [65536, 2048], P(('grp', 'seq'))
- gain_grads: float32 [4, 2048], replicated
The draws below stay inside these ranges and needn't reach their ends.
All inputs are finite; a program needn't handle non-finite values.
Results may differ from the reference program's by a relative error of at most 0.019.
Values may be sent and summed in bfloat16 or wider, within the bound.
A program may use at most 64 MiB of HBM per device.

```python
import jax
import jax.numpy as jnp
from jax import lax

D = 2048
HEADS = 16
TOK_DEV = 128
WINDOW = 128
SHORTEN = 16
TOKENS = 65536


def draw_tokens(key, part):
    values = jnp.clip(jax.random.normal(jax.random.fold_in(key, 1), (TOKENS, D), jnp.float32), -6.0, 6.0)
    return values.astype(jnp.bfloat16)


def gain_draw(key, salt, spread):
    values = spread * jnp.clip(jax.random.normal(jax.random.fold_in(key, salt), (D,), jnp.float32), -6.0, 6.0)
    return values.astype(jnp.float32)


def draw_query_gain(key, part):
    return gain_draw(key, 3, 1.0)


def draw_key_gain(key, part):
    return gain_draw(key, 4, 1.0)


def draw_short_query_gain(key, part):
    return gain_draw(key, 5, 4.0)


def draw_short_key_gain(key, part):
    return gain_draw(key, 6, 4.0)


def levels(stream_key, extent, pieces, least, high):
    loudness = 1.0
    for position, blocks in pieces:
        draws = jax.random.uniform(jax.random.fold_in(jax.random.fold_in(stream_key, 6), position), (blocks,), jnp.float32, least / len(pieces), high / len(pieces))
        loudness = loudness * jnp.repeat(jnp.exp(draws), extent[position] // blocks).reshape((-1,) + (1,) * (len(extent) - 1 - position))
    return loudness


def noise(key, dims, scale, reach, pieces=(), kind=jnp.bfloat16):
    values = jax.random.normal(key, dims, jnp.float32) * scale
    if len(pieces) > 0:
        values = levels(key, dims, pieces, -0.22, 0.18) * values
    return jnp.clip(values, min=-reach, max=reach).astype(kind)


def setup_inputs(seed: int = 0) -> dict:
    key_of = jax.random.split(jax.random.key(seed), 7)
    return {
        "tokens": draw_tokens(jax.random.fold_in(key_of[6], 71), 0),
        "grad_output": noise(key_of[1], (TOKENS, D), 1.0, 6.0, ((0, 512),)),
        "query_gain": draw_query_gain(jax.random.fold_in(key_of[6], 71), 0),
        "key_gain": draw_key_gain(jax.random.fold_in(key_of[6], 71), 0),
        "short_query_gain": draw_short_query_gain(jax.random.fold_in(key_of[6], 71), 0),
        "short_key_gain": draw_short_key_gain(jax.random.fold_in(key_of[6], 71), 0),
    }


def rounded(values):
    return lax.optimization_barrier(values.astype(jnp.bfloat16)).astype(jnp.float32)


def attention_weights(queries, key_rows, allowed):
    temper = queries.shape[-1] ** -0.5
    scores = jnp.einsum("qhe,khe->hqk", queries.astype(jnp.float32), key_rows.astype(jnp.float32)) * temper
    scores = jnp.where(allowed[None], scores, -1e30)
    log_total = jax.nn.logsumexp(scores, axis=-1)
    return jnp.where(allowed[None], jnp.exp(scores - log_total[..., None]), 0.0)


def attention_output(queries, key_rows, value_rows, allowed):
    weights = attention_weights(queries, key_rows, allowed)
    return jnp.einsum("hqk,khe->qhe", rounded(weights), value_rows.astype(jnp.float32))


def attention_grads(queries, key_rows, value_rows, incoming, allowed):
    temper = queries.shape[-1] ** -0.5
    weights = attention_weights(queries, key_rows, allowed)
    incoming_f = incoming.astype(jnp.float32)
    grad_weights = jnp.einsum("qhe,khe->hqk", incoming_f, value_rows.astype(jnp.float32))
    row_dot = jnp.sum(weights * grad_weights, axis=-1, keepdims=True)
    grad_scores = rounded(weights * (grad_weights - row_dot))
    grad_queries = jnp.einsum("hqk,khe->qhe", grad_scores, key_rows.astype(jnp.float32)) * temper
    grad_keys = jnp.einsum("hqk,qhe->khe", grad_scores, queries.astype(jnp.float32)) * temper
    grad_values = jnp.einsum("hqk,qhe->khe", rounded(weights), incoming_f)
    return grad_queries, grad_keys, grad_values


def reference(tokens, grad_output, query_gain, key_gain, short_query_gain, short_key_gain):
    length = tokens.shape[0]
    model_width = tokens.shape[1]
    head_size = model_width // HEADS
    blocks = length // TOK_DEV
    token_f = tokens.astype(jnp.float32)
    query_heads = (token_f * query_gain).astype(jnp.bfloat16).reshape(length, HEADS, head_size)
    key_heads = (token_f * key_gain).astype(jnp.bfloat16).reshape(length, HEADS, head_size)
    value_heads = tokens.reshape(length, HEADS, head_size)
    padding = jnp.zeros((WINDOW, HEADS, head_size), jnp.bfloat16)
    keys_padded = jnp.concatenate([padding, key_heads], axis=0)
    values_padded = jnp.concatenate([padding, value_heads], axis=0)

    def local_allowed(base):
        query_pos = base + jnp.arange(TOK_DEV, dtype=jnp.int32)[:, None]
        key_pos = base - WINDOW + jnp.arange(TOK_DEV + WINDOW, dtype=jnp.int32)[None, :]
        return (key_pos <= query_pos) & (key_pos > query_pos - WINDOW) & (key_pos >= 0)

    def block_inputs(block):
        base = (block * TOK_DEV).astype(jnp.int32)
        queries = lax.dynamic_slice_in_dim(query_heads, base, TOK_DEV, 0)
        key_rows = lax.dynamic_slice_in_dim(keys_padded, base, TOK_DEV + WINDOW, 0)
        value_rows = lax.dynamic_slice_in_dim(values_padded, base, TOK_DEV + WINDOW, 0)
        return base, queries, key_rows, value_rows

    def forward_block(block):
        base, queries, key_rows, value_rows = block_inputs(block)
        return attention_output(queries, key_rows, value_rows, local_allowed(base))

    starts = jnp.arange(blocks, dtype=jnp.int32)
    local_out = lax.map(forward_block, starts).reshape(length, model_width)
    mixed_rows = (token_f + local_out).astype(jnp.bfloat16)
    shifted = jnp.concatenate([jnp.zeros((SHORTEN - 1, model_width), jnp.bfloat16), mixed_rows], axis=0)[:length]
    short_len = length // SHORTEN
    pooled = (shifted.astype(jnp.float32).reshape(short_len, SHORTEN, model_width).sum(axis=1) * (1.0 / SHORTEN)).astype(jnp.bfloat16)
    grad_short = grad_output.astype(jnp.float32).reshape(short_len, SHORTEN, model_width).sum(axis=1).astype(jnp.bfloat16)
    pooled_f = pooled.astype(jnp.float32)
    short_queries = (pooled_f * short_query_gain).astype(jnp.bfloat16).reshape(short_len, HEADS, head_size)
    short_keys = (pooled_f * short_key_gain).astype(jnp.bfloat16).reshape(short_len, HEADS, head_size)
    short_values = pooled.reshape(short_len, HEADS, head_size)
    short_incoming = grad_short.reshape(short_len, HEADS, head_size)
    causal = jnp.arange(short_len, dtype=jnp.int32)[:, None] >= jnp.arange(short_len, dtype=jnp.int32)[None, :]

    def short_head(inputs):
        queries, key_rows, value_rows, incoming = inputs
        grads = attention_grads(queries[:, None], key_rows[:, None], value_rows[:, None], incoming[:, None], causal)
        return grads[0][:, 0], grads[1][:, 0], grads[2][:, 0]

    def by_head(values):
        return jnp.transpose(values, (1, 0, 2))

    def by_row(values):
        return jnp.transpose(values, (1, 0, 2)).reshape(short_len, model_width)

    short_gq, short_gk, short_gv = lax.map(short_head, (by_head(short_queries), by_head(short_keys), by_head(short_values), by_head(short_incoming)))
    short_gq = by_row(short_gq)
    short_gk = by_row(short_gk)
    short_gv = by_row(short_gv)
    grad_pooled = grad_short.astype(jnp.float32) + short_gq * short_query_gain + short_gk * short_key_gain + short_gv
    grad_short_query = jnp.sum(short_gq * pooled_f, axis=0)
    grad_short_key = jnp.sum(short_gk * pooled_f, axis=0)
    grad_following = jnp.concatenate([grad_pooled[1:], jnp.zeros((1, model_width), jnp.float32)], axis=0)
    spread = jnp.concatenate([grad_pooled[:, None], jnp.broadcast_to(grad_following[:, None], (short_len, SHORTEN - 1, model_width))], axis=1) * (1.0 / SHORTEN)
    grad_mixed = grad_output.astype(jnp.float32) + spread.reshape(length, model_width)
    incoming_heads = grad_mixed.astype(jnp.bfloat16).reshape(length, HEADS, head_size)

    def backward_block(block):
        base, queries, key_rows, value_rows = block_inputs(block)
        incoming = lax.dynamic_slice_in_dim(incoming_heads, base, TOK_DEV, 0)
        return attention_grads(queries, key_rows, value_rows, incoming, local_allowed(base))

    local_gq, local_gk, local_gv = lax.map(backward_block, starts)

    def settle(grads):
        own_rows = grads[:, WINDOW:]
        carried = jnp.concatenate([grads[1:, :WINDOW], jnp.zeros_like(grads[:1, :WINDOW])], axis=0)
        own_rows = own_rows.at[:, TOK_DEV - WINDOW:].add(carried)
        return own_rows.reshape(length, model_width)

    local_gq = local_gq.reshape(length, model_width)
    local_gk = settle(local_gk)
    local_gv = settle(local_gv)
    grad_tokens = (grad_mixed + local_gq * query_gain + local_gk * key_gain + local_gv).astype(jnp.bfloat16)
    gain_grads = jnp.stack([jnp.sum(local_gq * token_f, axis=0), jnp.sum(local_gk * token_f, axis=0), grad_short_query, grad_short_key]) * (length ** -0.5)
    return grad_tokens, gain_grads.astype(jnp.float32)
```

```python
import functools

import jax
import jax.numpy as jnp
from jax import lax
from jax.experimental import pallas as pl
from jax.experimental.pallas import tpu as pltpu
from jax.sharding import Mesh
from jax.sharding import PartitionSpec as P

AXES = ("zh", "y", "x", "zl", "c")
MESH = pl.DeviceIdType.MESH
T = 128
HD = 128
SLOTS = 8
NEGATIVE = -1e30
TEMPER = HD ** (-0.5)
F32 = jnp.float32
BF16 = jnp.bfloat16
GROUP = 4


def mm(a, b):
    return jnp.dot(a, b, preferred_element_type=F32)


def mm_nt(a, b):
    return lax.dot_general(a, b, (((1,), (1,)), ((), ())), preferred_element_type=F32)


def mm_tn(a, b):
    return lax.dot_general(a, b, (((0,), (0,)), ((), ())), preferred_element_type=F32)


def iota(shape, dim):
    return lax.broadcasted_iota(jnp.int32, shape, dim)


def remote(src, dst, send, recv, device):
    return pltpu.make_async_remote_copy(
        src_ref=src, dst_ref=dst, send_sem=send, recv_sem=recv, device_id=device, device_id_type=MESH
    )


def loop(count, body, start=0):
    def step(k, carry):
        body(k)
        return carry

    lax.fori_loop(start, count, step, 0)


def kernel(
    sizes,
    tok, gout, qg, kg, sqg, skg,
    out, gains,
    ctx, gsrc, tnext, wt, pg_send, pg_recv, pgx, kz, prob, dprob, dk, dv, stats,
    qgr_send, qgr_recv, kgr_send, kgr_recv, gp_send, gp_recv, gp_prev,
    ret_send, ret_recv, acc, outv, gr_send, gr_recv, gx, gz, gfin,
    load_sem, next_send, next_recv, tok_send, tok_recv, a_send, a_recv, x_send, x_recv, z_send, z_recv,
    prev_send, prev_recv,
):
    nzh, ny, nx, nzl, nc = sizes
    nz, na = nzh * nzl, ny * nc
    heads = na
    span = na * SLOTS
    zh, y, x, zl, c = [lax.axis_index(name) for name in AXES]
    z = zh * nzl + zl
    a = y * nc + c
    chain = (((zh * ny + y) * nx + x) * nzl + zl) * nc + c
    total = nzh * ny * nx * nzl * nc

    def decode(index):
        return (
            index // (ny * nx * nzl * nc),
            index // (nx * nzl * nc) % ny,
            index // (nzl * nc) % nx,
            index // nc % nzl,
            index % nc,
        )

    following = decode((chain + 1) % total)
    previous = decode((chain + total - 1) % total)

    def at_a(other):
        return (zh, other // nc, x, zl, other % nc)

    def at_x(other):
        return (zh, y, other, zl, c)

    def at_z(other):
        return (other // nzl, y, x, other % nzl, c)

    barrier = pltpu.get_barrier_semaphore()

    def greet(device):
        pl.semaphore_signal(barrier, inc=1, device_id=device, device_id_type=MESH)

    greet(following)
    greet(previous)
    loop(na, lambda k: greet(at_a((a + k) % na)), 1)
    loop(nz, lambda k: greet(at_z((z + k) % nz)), 1)
    loop(nx, lambda k: greet(at_x((x + k) % nx)), 1)

    load_tok = pltpu.make_async_copy(tok, ctx.at[pl.ds(T, T)], load_sem.at[0])
    load_gout = pltpu.make_async_copy(gout, gsrc.at[pl.ds(0, T)], load_sem.at[1])
    load_tok.start()
    load_gout.start()

    pl.semaphore_wait(barrier, 2 + (na - 1) + (nz - 1) + (nx - 1))

    def columns(h):
        return pl.ds(pl.multiple_of(h * HD, HD), HD)

    head_tok = remote(tok.at[pl.ds(0, 16)], tnext, next_send.at[0], next_recv.at[0], previous)
    head_gout = remote(gout.at[pl.ds(0, 16)], gsrc.at[pl.ds(T, 16)], next_send.at[1], next_recv.at[1], previous)
    head_tok.start()
    head_gout.start()

    def tokens_of(h):
        return remote(
            tok.at[:, columns(h)], ctx.at[pl.ds(0, T), columns(h)], tok_send.at[h], tok_recv.at[h], following
        )

    loop(heads, lambda h: tokens_of(h).start())

    load_tok.wait()
    load_gout.wait()
    head_tok.wait_recv()
    head_gout.wait_recv()

    key_row = iota((T, T), 0)
    query_col = iota((T, T), 1)
    prior = key_row > query_col
    first_bias = jnp.where(chain == 0, NEGATIVE, 0.0)
    last_bias = jnp.where(chain == total - 1, NEGATIVE, 0.0)
    not_last = jnp.where(chain == total - 1, 0.0, 1.0)
    top_row = iota((T, HD), 0) == 0
    ext_bias = jnp.where(iota((T, 16), 0) == 0, 0.0, last_bias)
    slot = iota((SLOTS, T), 0)
    row = iota((SLOTS, T), 1)
    keep = jnp.where(slot == SLOTS - 1, not_last, 1.0)
    pool = jnp.where((row > slot * 16) & (row <= slot * 16 + 16), keep, 0.0).astype(BF16)
    gpool = jnp.where((row >= slot * 16 + 16) & (row < slot * 16 + 32), 1.0, 0.0).astype(BF16)
    tail = iota((SLOTS, HD), 0) == SLOTS - 1

    def exchange(kind, h):
        send, recv, ssem, rsem = kind
        return remote(send.at[h], recv.at[a], ssem.at[h], rsem.at[a], at_a(h))

    def arrived(kind, h):
        send, recv, ssem, rsem = kind
        remote(send.at[h], recv.at[h], ssem.at[h], rsem.at[h], at_a(h)).wait_recv()

    def others_a(body):
        loop(na, lambda k: body((a + k) % na), 1)

    pg_kind = (pg_send, pg_recv, a_send.at[0], a_recv.at[0])
    gp_kind = (gp_send, gp_recv, a_send.at[1], a_recv.at[1])
    gr_kind = (gr_send, gr_recv, a_send.at[2], a_recv.at[2])

    def forward(h):
        cols = columns(h)
        both = ctx[:, cols]
        both_f = both.astype(F32)
        own_f = both_f[T:]
        gq, gk = qg[:, cols], kg[:, cols]
        queries = (own_f * gq).astype(BF16)
        keys = (both_f * gk).astype(BF16)
        scores = mm_nt(keys, queries) * TEMPER
        scores = jnp.where(prior, scores[:T] + first_bias, scores[T:])
        weights = jnp.exp(scores - scores.max(axis=0, keepdims=True))
        weights = weights * (1.0 / weights.sum(axis=0, keepdims=True))
        wt[h] = weights
        split = jnp.concatenate([jnp.where(prior, weights, 0.0), jnp.where(prior, 0.0, weights)], axis=0)
        mixed = (own_f + mm_tn(split.astype(BF16), both)).astype(BF16)
        ext_f = tnext[:, cols].astype(F32)
        ext_values = jnp.where(top_row, ext_f[0:1], own_f)
        ext_queries = (ext_f * gq).astype(BF16)
        ext_keys = (ext_values * gk).astype(BF16)
        ext_scores = mm_nt(ext_keys, ext_queries) * TEMPER + ext_bias
        ext_weights = jnp.exp(ext_scores - ext_scores.max(axis=0, keepdims=True))
        ext_weights = ext_weights * (1.0 / ext_weights.sum(axis=0, keepdims=True))
        ext_mixed = (ext_f + mm_tn(ext_weights.astype(BF16), ext_values.astype(BF16))).astype(BF16)
        pooled = mm(pool, mixed) + jnp.where(tail, ext_mixed.astype(F32)[0:1], 0.0)
        incoming = gsrc[pl.ds(0, T), cols]
        short = mm(gpool, incoming)
        next_sum = gsrc[pl.ds(T, 16), cols].astype(F32).sum(axis=0, keepdims=True)
        short = short + jnp.where(tail, next_sum, 0.0)
        pg_send[h] = jnp.concatenate([pooled * (1.0 / 16), short], axis=0).astype(BF16)

        @pl.when(h != a)
        def _():
            exchange(pg_kind, h).start()

        @pl.when(h == a)
        def _():
            pg_recv[h] = pg_send[h]

    def forward_group(g):
        for u in range(GROUP):
            tokens_of(g * GROUP + u).wait_recv()
        for u in range(GROUP):
            forward(g * GROUP + u)

    loop(heads // GROUP, forward_group)
    others_a(lambda h: arrived(pg_kind, h))

    blocks = pg_recv[...].astype(F32)
    pooled_own = blocks[:, :SLOTS].reshape(span, HD).astype(BF16)
    short_own = blocks[:, SLOTS:].reshape(span, HD)
    pgx[x, 0] = pooled_own
    pgx[x, 1] = short_own.astype(BF16)
    kz[z] = pooled_own

    def gather_x(other):
        return remote(pgx.at[x], pgx.at[x], x_send.at[0, other], x_recv.at[0, x], at_x(other))

    def gather_z(other):
        return remote(kz.at[z], kz.at[z], z_send.at[0, other], z_recv.at[0, z], at_z(other))

    def others_x(body):
        loop(nx, lambda k: body((x + k) % nx), 1)

    def others_z(body):
        loop(nz, lambda k: body((z + k) % nz), 1)

    others_z(lambda o: gather_z(o).start())
    others_x(lambda o: gather_x(o).start())

    def x_arrived(phase, ref, other):
        remote(ref.at[other], ref.at[other], x_send.at[phase, other], x_recv.at[phase, other], at_x(other)).wait_recv()

    def z_arrived(phase, ref, other):
        remote(ref.at[other], ref.at[other], z_send.at[phase, other], z_recv.at[phase, other], at_z(other)).wait_recv()

    def position(zi, xi, index):
        source, place = index // SLOTS, index % SLOTS
        device = ((zi // nzl * ny + source // nc) * nx + xi) * nzl * nc + zi % nzl * nc + source % nc
        raw = device * SLOTS + place + 1
        return jnp.where(raw == total * SLOTS, 0, raw)

    head_cols = columns(a)
    gain_query = sqg[:, head_cols]
    gain_key = skg[:, head_cols]

    others_z(lambda o: z_arrived(0, kz, o))
    others_x(lambda o: x_arrived(0, pgx, o))

    count = nz * span
    values = kz[...].reshape(count, HD)
    short_keys = (values.astype(F32) * gain_key).astype(BF16)
    key_index = iota((count, 1), 0)
    key_pos = position(key_index // span, x, key_index % span)

    def first_pass(b):
        queries = (pgx[b, 0].astype(F32) * gain_query).astype(BF16)
        query_pos = position(z, b, iota((1, span), 1))
        visible = key_pos <= query_pos
        scores = jnp.where(visible, mm_nt(short_keys, queries) * TEMPER, NEGATIVE)
        highest = jnp.maximum(scores.max(axis=0, keepdims=True), 0.1 * NEGATIVE)
        weights = jnp.exp(scores - highest)
        grads = mm_nt(values, pgx[b, 1])
        prob[b] = weights
        dprob[b] = grads
        sums = weights.sum(axis=0, keepdims=True)
        dots = (weights * grads).sum(axis=0, keepdims=True)
        stats[x, b] = jnp.concatenate([highest, sums, dots, jnp.zeros((5, span), F32)], axis=0)

    loop(nx, first_pass)

    def send_stats(other):
        return remote(stats.at[x], stats.at[x], x_send.at[1, other], x_recv.at[1, x], at_x(other))

    others_x(lambda o: send_stats(o).start())
    dk[...] = jnp.zeros_like(dk)
    dv[...] = jnp.zeros_like(dv)
    others_x(lambda o: x_arrived(1, stats, o))

    def send_query(other):
        return remote(qgr_send.at[other], qgr_recv.at[x], x_send.at[2, other], x_recv.at[2, x], at_x(other))

    def send_key(other):
        return remote(kgr_send.at[other], kgr_recv.at[z], z_send.at[1, other], z_recv.at[1, z], at_z(other))

    gr_short = jnp.zeros((1, HD), F32)

    def second_pass(b, gain_sum):
        pieces = [stats[s, b] for s in range(nx)]
        top = pieces[0][0:1]
        for piece in pieces[1:]:
            top = jnp.maximum(top, piece[0:1])
        sums = jnp.zeros((1, span), F32)
        dots = jnp.zeros((1, span), F32)
        for piece in pieces:
            factor = jnp.exp(piece[0:1] - top)
            sums = sums + piece[1:2] * factor
            dots = dots + piece[2:3] * factor
        inverse = 1.0 / sums
        mine = jnp.exp(stats[x, b][0:1] - top) * inverse
        dots = dots * inverse
        weights = prob[b] * mine
        ds = (weights * (dprob[b] - dots)).astype(BF16)
        pooled_f = pgx[b, 0].astype(F32)
        queries = (pooled_f * gain_query).astype(BF16)
        dk[...] += mm(ds, queries)
        dv[...] += mm(weights.astype(BF16), pgx[b, 1])
        grad_q = mm_tn(ds, short_keys) * TEMPER
        qgr_send[b] = (grad_q * gain_query).astype(BF16)

        @pl.when(b != x)
        def _():
            send_query(b).start()

        @pl.when(b == x)
        def _():
            qgr_recv[b] = qgr_send[b]

        return gain_sum + (grad_q * pooled_f).sum(axis=0, keepdims=True)

    gain_short_query = lax.fori_loop(0, nx, second_pass, gr_short)
    grad_k = dk[...] * TEMPER
    gain_short_key = (grad_k * values.astype(F32)).sum(axis=0, keepdims=True)
    kgr_send[...] = (grad_k * gain_key + dv[...]).astype(BF16).reshape(nz, span, HD)
    others_z(lambda o: send_key(o).start())
    kgr_recv[z] = kgr_send[z]
    others_x(lambda o: x_arrived(2, qgr_recv, o))
    others_z(lambda o: z_arrived(1, kgr_recv, o))
    grad_pooled = short_own + qgr_recv[...].astype(F32).sum(axis=0) + kgr_recv[...].astype(F32).sum(axis=0)
    gp_send[...] = grad_pooled.reshape(na, SLOTS, HD)
    others_a(lambda h: exchange(gp_kind, h).start())
    gp_recv[a] = gp_send[a]
    others_a(lambda h: arrived(gp_kind, h))
    pass_on = remote(gp_recv, gp_prev, next_send.at[2], next_recv.at[2], following)
    pass_on.start()
    pass_on.wait_recv()

    token = iota((T, 16), 0)
    place = iota((T, 16), 1)
    source = jnp.where(token == 0, 15, (token + 15) // 16 - 1)
    spread = jnp.where(place == source, jnp.where(place == SLOTS - 1, not_last, 1.0) * (1.0 / 16), 0.0).astype(BF16)

    def give_back(h):
        return remote(ret_send.at[h], ret_recv.at[h], prev_send.at[h], prev_recv.at[h], previous)

    def backward(h):
        cols = columns(h)
        both = ctx[:, cols]
        both_f = both.astype(F32)
        own_f = both_f[T:]
        gq, gk = qg[:, cols], kg[:, cols]
        queries = (own_f * gq).astype(BF16)
        keys = (both_f * gk).astype(BF16)
        rows = jnp.concatenate([gp_recv[h], gp_prev[h]], axis=0).astype(BF16)
        grad_mixed = gsrc[pl.ds(0, T), cols].astype(F32) + mm(spread, rows)
        incoming = grad_mixed.astype(BF16)
        grads = mm_nt(both, incoming)
        grads = jnp.where(prior, grads[:T], grads[T:])
        weights = wt[h]
        dots = (weights * grads).sum(axis=0, keepdims=True)
        ds = weights * (grads - dots)
        ds = jnp.concatenate([jnp.where(prior, ds, 0.0), jnp.where(prior, 0.0, ds)], axis=0).astype(BF16)
        split = jnp.concatenate([jnp.where(prior, weights, 0.0), jnp.where(prior, 0.0, weights)], axis=0).astype(BF16)
        grad_q = mm_tn(ds, keys) * TEMPER
        grad_k = mm(ds, queries) * TEMPER
        to_keys = grad_k * gk + mm(split, incoming)
        ret_send[h] = to_keys[:T].astype(BF16)
        give_back(h).start()
        acc[h] = grad_mixed + grad_q * gq + to_keys[T:]
        sum_q = (grad_q * own_f).sum(axis=0, keepdims=True)
        sum_k = (grad_k * both_f).sum(axis=0, keepdims=True)
        gr_send[h] = jnp.concatenate([sum_q, sum_k, jnp.zeros((6, HD), F32)], axis=0)

        @pl.when(h != a)
        def _():
            exchange(gr_kind, h).start()

        @pl.when(h == a)
        def _():
            gr_recv[h] = gr_send[h]

    def backward_group(g):
        for u in range(GROUP):
            backward(g * GROUP + u)

    loop(heads // GROUP, backward_group)

    def finish(h):
        give_back(h).wait_recv()
        outv[:, columns(h)] = (acc[h] + ret_recv[h].astype(F32)).astype(BF16)

    loop(heads, finish)
    store = pltpu.make_async_copy(outv, out, load_sem.at[2])
    store.start()

    others_a(lambda h: arrived(gr_kind, h))
    short_rows = jnp.concatenate([jnp.zeros((2, HD), F32), gain_short_query, gain_short_key, jnp.zeros((4, HD), F32)], axis=0)
    gx[x] = gr_recv[...].sum(axis=0) + short_rows

    def sum_x(other):
        return remote(gx.at[x], gx.at[x], x_send.at[3, other], x_recv.at[3, x], at_x(other))

    def sum_z(other):
        return remote(gz.at[z], gz.at[z], z_send.at[2, other], z_recv.at[2, z], at_z(other))

    def share(other):
        return remote(gfin.at[a], gfin.at[a], a_send.at[3, other], a_recv.at[3, a], at_a(other))

    others_x(lambda o: sum_x(o).start())
    others_x(lambda o: x_arrived(3, gx, o))
    gz[z] = gx[...].sum(axis=0)
    others_z(lambda o: sum_z(o).start())
    others_z(lambda o: z_arrived(2, gz, o))
    gfin[a] = gz[...].sum(axis=0) * (float(total * T) ** (-0.5))
    others_a(lambda h: share(h).start())
    others_a(
        lambda h: remote(gfin.at[h], gfin.at[h], a_send.at[3, h], a_recv.at[3, h], at_a(h)).wait_recv()
    )

    def put(h):
        gains[:, columns(h)] = gfin[h][0:4]

    loop(heads, put)

    head_tok.wait_send()
    head_gout.wait_send()
    pass_on.wait_send()

    def drain(h):
        tokens_of(h).wait_send()
        give_back(h).wait_send()

    loop(heads, drain)

    def drain_a(h):
        exchange(pg_kind, h).wait_send()
        exchange(gp_kind, h).wait_send()
        exchange(gr_kind, h).wait_send()
        share(h).wait_send()

    others_a(drain_a)

    def drain_x(o):
        gather_x(o).wait_send()
        send_stats(o).wait_send()
        send_query(o).wait_send()
        sum_x(o).wait_send()

    others_x(drain_x)

    def drain_z(o):
        gather_z(o).wait_send()
        send_key(o).wait_send()
        sum_z(o).wait_send()

    others_z(drain_z)
    store.wait()


def shards(sizes, tokens, grad_output, query_gain, key_gain, short_query_gain, short_key_gain):
    nzh, ny, nx, nzl, nc = sizes
    nz, na = nzh * nzl, ny * nc
    width = tokens.shape[1]
    heads = width // HD
    span = na * SLOTS
    vmem = pl.BlockSpec(memory_space=pltpu.VMEM)
    hbm = pl.BlockSpec(memory_space=pl.ANY)
    dma = pltpu.SemaphoreType.DMA
    scratch = [
        pltpu.VMEM((2 * T, width), BF16),
        pltpu.VMEM((T + 16, width), BF16),
        pltpu.VMEM((16, width), BF16),
        pltpu.VMEM((heads, T, T), F32),
        pltpu.VMEM((na, 16, HD), BF16),
        pltpu.VMEM((na, 16, HD), BF16),
        pltpu.VMEM((nx, 2, span, HD), BF16),
        pltpu.VMEM((nz, span, HD), BF16),
        pltpu.VMEM((nx, nz * span, span), F32),
        pltpu.VMEM((nx, nz * span, span), F32),
        pltpu.VMEM((nz * span, HD), F32),
        pltpu.VMEM((nz * span, HD), F32),
        pltpu.VMEM((nx, nx, 8, span), F32),
        pltpu.VMEM((nx, span, HD), BF16),
        pltpu.VMEM((nx, span, HD), BF16),
        pltpu.VMEM((nz, span, HD), BF16),
        pltpu.VMEM((nz, span, HD), BF16),
        pltpu.VMEM((na, SLOTS, HD), F32),
        pltpu.VMEM((na, SLOTS, HD), F32),
        pltpu.VMEM((na, SLOTS, HD), F32),
        pltpu.VMEM((heads, T, HD), BF16),
        pltpu.VMEM((heads, T, HD), BF16),
        pltpu.VMEM((heads, T, HD), F32),
        pltpu.VMEM((T, width), BF16),
        pltpu.VMEM((na, 8, HD), F32),
        pltpu.VMEM((na, 8, HD), F32),
        pltpu.VMEM((nx, 8, HD), F32),
        pltpu.VMEM((nz, 8, HD), F32),
        pltpu.VMEM((na, 8, HD), F32),
        dma((3,)),
        dma((3,)),
        dma((3,)),
        dma((heads,)),
        dma((heads,)),
        dma((4, na)),
        dma((4, na)),
        dma((4, nx)),
        dma((4, nx)),
        dma((3, nz)),
        dma((3, nz)),
        dma((heads,)),
        dma((heads,)),
    ]
    return pl.pallas_call(
        functools.partial(kernel, sizes),
        out_shape=(
            jax.ShapeDtypeStruct(tokens.shape, BF16),
            jax.ShapeDtypeStruct((4, width), F32),
        ),
        in_specs=[hbm, hbm, vmem, vmem, vmem, vmem],
        out_specs=(hbm, vmem),
        scratch_shapes=scratch,
        compiler_params=pltpu.CompilerParams(collective_id=0, has_side_effects=True),
        name="hourglass",
    )(
        tokens,
        grad_output,
        query_gain.reshape(1, width),
        key_gain.reshape(1, width),
        short_query_gain.reshape(1, width),
        short_key_gain.reshape(1, width),
    )


def build(mesh, sizes):
    finer = Mesh(mesh.devices.reshape(sizes), AXES)
    return jax.shard_map(
        functools.partial(shards, sizes),
        mesh=finer,
        in_specs=(P(AXES, None), P(AXES, None), P(), P(), P(), P()),
        out_specs=(P(AXES, None), P()),
        check_vma=False,
    )


def solution(mesh):
    return build(mesh, (2, 8, 4, 4, 2))
```

```python
import functools

import jax
import jax.numpy as jnp
from jax import lax
from jax.experimental import pallas as pl
from jax.experimental.pallas import tpu as pltpu
from jax.sharding import Mesh
from jax.sharding import PartitionSpec as P

AXES = ("zh", "y", "x", "zl", "c")
MESH = pl.DeviceIdType.MESH
T = 128
HD = 128
SLOTS = 8
NEGATIVE = -1e30
TEMPER = HD ** (-0.5)
F32 = jnp.float32
BF16 = jnp.bfloat16
GROUP = 4


def mm(a, b):
    return jnp.dot(a, b, preferred_element_type=F32)


def mm_nt(a, b):
    return lax.dot_general(a, b, (((1,), (1,)), ((), ())), preferred_element_type=F32)


def mm_tn(a, b):
    return lax.dot_general(a, b, (((0,), (0,)), ((), ())), preferred_element_type=F32)


def iota(shape, dim):
    return lax.broadcasted_iota(jnp.int32, shape, dim)


def remote(src, dst, send, recv, device):
    return pltpu.make_async_remote_copy(
        src_ref=src, dst_ref=dst, send_sem=send, recv_sem=recv, device_id=device, device_id_type=MESH
    )


def loop(count, body, start=0):
    def step(k, carry):
        body(k)
        return carry

    lax.fori_loop(start, count, step, 0)


def kernel(
    sizes,
    tok, gout, qg, kg, sqg, skg,
    out, gains,
    ctx, gsrc, tnext, qs, ks, own_scores, short, ext, wt, ws, pg_send, pg_recv, pgx, kz, prob, dprob, ds_short, stats,
    qgr_send, qgr_recv, kgr_send, kgr_recv, gp_send, gp_recv, gp_prev,
    gm, ds_local, gk_local, ret_send, ret_recv, acc, outv, gr_send, gr_recv, gx, gz, gfin,
    load_sem, next_send, next_recv, tok_send, tok_recv, a_send, a_recv, x_send, x_recv, z_send, z_recv,
    prev_send, prev_recv,
):
    nzh, ny, nx, nzl, nc = sizes
    nz, na = nzh * nzl, ny * nc
    heads = na
    span = na * SLOTS
    zh, y, x, zl, c = [lax.axis_index(name) for name in AXES]
    z = zh * nzl + zl
    a = y * nc + c
    chain = (((zh * ny + y) * nx + x) * nzl + zl) * nc + c
    total = nzh * ny * nx * nzl * nc

    def decode(index):
        return (
            index // (ny * nx * nzl * nc),
            index // (nx * nzl * nc) % ny,
            index // (nzl * nc) % nx,
            index // nc % nzl,
            index % nc,
        )

    following = decode((chain + 1) % total)
    previous = decode((chain + total - 1) % total)

    def at_a(other):
        return (zh, other // nc, x, zl, other % nc)

    def at_x(other):
        return (zh, y, other, zl, c)

    def at_z(other):
        return (other // nzl, y, x, other % nzl, c)

    barrier = pltpu.get_barrier_semaphore()
    drains = []

    def greet(device):
        pl.semaphore_signal(barrier, inc=1, device_id=device, device_id_type=MESH)

    greet(following)
    greet(previous)
    loop(na, lambda k: greet(at_a((a + k) % na)), 1)
    loop(nz, lambda k: greet(at_z((z + k) % nz)), 1)
    loop(nx, lambda k: greet(at_x((x + k) % nx)), 1)

    load_tok = pltpu.make_async_copy(tok, ctx.at[pl.ds(T, T)], load_sem.at[0])
    load_gout = pltpu.make_async_copy(gout, gsrc.at[pl.ds(0, T)], load_sem.at[1])
    load_tok.start()
    load_gout.start()

    pl.semaphore_wait(barrier, 2 + (na - 1) + (nz - 1) + (nx - 1))

    def columns(h):
        return pl.ds(pl.multiple_of(h * HD, HD), HD)

    head_tok = remote(tok.at[pl.ds(0, 16)], tnext, next_send.at[0], next_recv.at[0], previous)
    head_gout = remote(gout.at[pl.ds(0, 16)], gsrc.at[pl.ds(T, 16)], next_send.at[1], next_recv.at[1], previous)
    head_tok.start()
    head_gout.start()
    drains.append(head_tok.wait_send)
    drains.append(head_gout.wait_send)

    def tokens_of(h):
        return remote(
            tok.at[:, columns(h)], ctx.at[pl.ds(0, T), columns(h)], tok_send.at[h], tok_recv.at[h], following
        )

    loop(heads, lambda h: tokens_of(h).start())
    drains.append(lambda: loop(heads, lambda h: tokens_of(h).wait_send()))

    key_row = iota((T, T), 0)
    query_col = iota((T, T), 1)
    prior = key_row > query_col
    first_bias = jnp.where(chain == 0, NEGATIVE, 0.0)
    last_bias = jnp.where(chain == total - 1, NEGATIVE, 0.0)
    not_last = jnp.where(chain == total - 1, 0.0, 1.0)
    self_lane = iota((SLOTS, T), 1) == 0
    slot = iota((SLOTS, T), 0)
    row = iota((SLOTS, T), 1)
    keep = jnp.where(slot == SLOTS - 1, not_last, 1.0)
    pool = jnp.where((row > slot * 16) & (row <= slot * 16 + 16), keep, 0.0).astype(BF16)
    gpool = jnp.where((row >= slot * 16 + 16) & (row < slot * 16 + 32), 1.0, 0.0).astype(BF16)
    tail = iota((SLOTS, HD), 0) == SLOTS - 1

    load_tok.wait()
    load_gout.wait()

    def grouped(body):
        def several(g):
            for u in range(GROUP):
                body(g * GROUP + u)

        loop(heads // GROUP, several)

    def prepare(h):
        cols = columns(h)
        own_f = ctx[pl.ds(T, T), cols].astype(F32)
        queries = (own_f * qg[:, cols]).astype(BF16)
        keys = (own_f * kg[:, cols]).astype(BF16)
        qs[h] = queries
        ks[h] = keys
        own_scores[h] = mm_nt(keys, queries) * TEMPER
        short[h] = mm(gpool, gsrc[pl.ds(0, T), cols])

    grouped(prepare)
    head_tok.wait_recv()
    head_gout.wait_recv()

    def extend(h):
        cols = columns(h)
        ext_f = tnext[:, cols].astype(F32)[:SLOTS]
        queries = (ext_f * qg[:, cols]).astype(BF16)
        keys = (ext_f * kg[:, cols]).astype(BF16)
        same = (queries.astype(F32) * keys.astype(F32)).sum(axis=1, keepdims=True) * TEMPER
        scores = jnp.where(self_lane, same, mm_nt(queries, ks[h]) * TEMPER + last_bias)
        weights = jnp.exp(scores - scores.max(axis=1, keepdims=True))
        weights = (weights * (1.0 / weights.sum(axis=1, keepdims=True))).astype(BF16).astype(F32)
        found = mm(jnp.where(self_lane, 0.0, weights).astype(BF16), ctx[pl.ds(T, T), cols])
        found = found + weights[:, 0:1] * ext_f
        ext[h] = (ext_f + found).astype(BF16).astype(F32)
        next_sum = gsrc[pl.ds(T, 16), cols].astype(F32).sum(axis=0, keepdims=True)
        short[h] += jnp.where(tail, next_sum, 0.0)

    grouped(extend)

    def exchange(kind, h):
        send, recv, ssem, rsem = kind
        return remote(send.at[h], recv.at[a], ssem.at[h], rsem.at[a], at_a(h))

    def arrived(kind, h):
        send, recv, ssem, rsem = kind
        remote(send.at[h], recv.at[h], ssem.at[h], rsem.at[h], at_a(h)).wait_recv()

    def others_a(body):
        loop(na, lambda k: body((a + k) % na), 1)

    pg_kind = (pg_send, pg_recv, a_send.at[0], a_recv.at[0])
    gp_kind = (gp_send, gp_recv, a_send.at[1], a_recv.at[1])
    gr_kind = (gr_send, gr_recv, a_send.at[2], a_recv.at[2])

    def forward(h):
        cols = columns(h)
        both = ctx[:, cols]
        both_f = both.astype(F32)
        keys = (both_f[:T] * kg[:, cols]).astype(BF16)
        scores = jnp.where(prior, mm_nt(keys, qs[h]) * TEMPER + first_bias, own_scores[h])
        weights = jnp.exp(scores - scores.max(axis=0, keepdims=True))
        weights = weights * (1.0 / weights.sum(axis=0, keepdims=True))
        wt[h] = weights
        split = jnp.concatenate([jnp.where(prior, weights, 0.0), jnp.where(prior, 0.0, weights)], axis=0).astype(BF16)
        ws[h] = split
        mixed = (both_f[T:] + mm_tn(split, both)).astype(BF16)
        pooled = mm(pool, mixed) + jnp.where(tail, ext[h][0:1], 0.0)
        pg_send[h] = jnp.concatenate([pooled * (1.0 / 16), short[h]], axis=0).astype(BF16)

        @pl.when(h != a)
        def _():
            exchange(pg_kind, h).start()

        @pl.when(h == a)
        def _():
            pg_recv[h] = pg_send[h]

    def forward_group(g):
        for u in range(GROUP):
            tokens_of(g * GROUP + u).wait_recv()
        for u in range(GROUP):
            forward(g * GROUP + u)

    loop(heads // GROUP, forward_group)
    others_a(lambda h: arrived(pg_kind, h))
    drains.append(lambda: others_a(lambda h: exchange(pg_kind, h).wait_send()))

    blocks = pg_recv[...].astype(F32)
    pooled_own = blocks[:, :SLOTS].reshape(span, HD).astype(BF16)
    short_own = blocks[:, SLOTS:].reshape(span, HD)
    pgx[x, 0] = pooled_own
    pgx[x, 1] = short_own.astype(BF16)
    kz[z] = pooled_own

    def gather_x(other):
        return remote(pgx.at[x], pgx.at[x], x_send.at[0, other], x_recv.at[0, x], at_x(other))

    def gather_z(other):
        return remote(kz.at[z], kz.at[z], z_send.at[0, other], z_recv.at[0, z], at_z(other))

    def others_x(body):
        loop(nx, lambda k: body((x + k) % nx), 1)

    def others_z(body):
        loop(nz, lambda k: body((z + k) % nz), 1)

    def zig(k):
        half = (k + 1) // 2
        return (z + nz + half * (1 - 2 * ((k + 1) % 2))) % nz

    loop(nz - 1, lambda k: gather_z(zig(nz - 1 - k)).start())
    others_x(lambda o: gather_x(o).start())

    def x_arrived(phase, ref, other):
        remote(ref.at[other], ref.at[other], x_send.at[phase, other], x_recv.at[phase, other], at_x(other)).wait_recv()

    def z_arrived(phase, ref, other):
        remote(ref.at[other], ref.at[other], z_send.at[phase, other], z_recv.at[phase, other], at_z(other)).wait_recv()

    def position(zi, xi, index):
        source, place = index // SLOTS, index % SLOTS
        device = ((zi // nzl * ny + source // nc) * nx + xi) * nzl * nc + zi % nzl * nc + source % nc
        raw = device * SLOTS + place + 1
        return jnp.where(raw == total * SLOTS, 0, raw)

    head_cols = columns(a)
    gain_query = sqg[:, head_cols]
    gain_key = skg[:, head_cols]

    gain_both = gain_query * gain_key * TEMPER
    others_x(lambda o: x_arrived(0, pgx, o))
    wide = nx * span
    pooled_all = pgx[:, 0].reshape(wide, HD)
    short_all = pgx[:, 1].reshape(wide, HD)
    queries_all = (pooled_all.astype(F32) * gain_query).astype(BF16)
    query_index = iota((1, wide), 1)
    query_pos = position(z, query_index // span, query_index % span)
    key_index = iota((span, 1), 0)

    def first_pass(k, highest):
        b = zig(k)

        @pl.when(k > 0)
        def _():
            z_arrived(0, kz, b)

        values = kz[b]
        keys = (values.astype(F32) * gain_key).astype(BF16)
        visible = position(b, x, key_index) <= query_pos
        scores = jnp.where(visible, mm_nt(keys, queries_all) * TEMPER, NEGATIVE)
        prob[b] = scores
        dprob[b] = mm_nt(values, short_all)
        return jnp.maximum(highest, scores.max(axis=0, keepdims=True))

    highest = lax.fori_loop(0, nz, first_pass, jnp.full((1, wide), 0.1 * NEGATIVE, F32))
    drains.append(lambda: others_z(lambda o: gather_z(o).wait_send()))
    drains.append(lambda: others_x(lambda o: gather_x(o).wait_send()))

    def totals(b, carry):
        sums, dots = carry
        weights = jnp.exp(prob[b] - highest)
        prob[b] = weights
        return (
            sums + weights.sum(axis=0, keepdims=True),
            dots + (weights * dprob[b]).sum(axis=0, keepdims=True),
        )

    zero = jnp.zeros((1, wide), F32)
    sums, dots = lax.fori_loop(0, nz, totals, (zero, zero))
    stats[x] = jnp.concatenate([highest, sums, dots, jnp.zeros((5, wide), F32)], axis=0)

    def send_stats(other):
        return remote(stats.at[x], stats.at[x], x_send.at[1, other], x_recv.at[1, x], at_x(other))

    others_x(lambda o: send_stats(o).start())
    others_x(lambda o: x_arrived(1, stats, o))
    drains.append(lambda: others_x(lambda o: send_stats(o).wait_send()))

    def send_query(other):
        return remote(qgr_send.at[other], qgr_recv.at[x], x_send.at[2, other], x_recv.at[2, x], at_x(other))

    def send_key(other):
        return remote(kgr_send.at[other], kgr_recv.at[z], z_send.at[1, other], z_recv.at[1, z], at_z(other))

    pieces = [stats[s] for s in range(nx)]
    top = pieces[0][0:1]
    for piece in pieces[1:]:
        top = jnp.maximum(top, piece[0:1])
    all_sums = jnp.zeros((1, wide), F32)
    all_dots = jnp.zeros((1, wide), F32)
    for piece in pieces:
        factor = jnp.exp(piece[0:1] - top)
        all_sums = all_sums + piece[1:2] * factor
        all_dots = all_dots + piece[2:3] * factor
    inverse = 1.0 / all_sums
    mine = jnp.exp(highest - top) * inverse
    all_dots = all_dots * inverse

    def second_pass(k, gain_sum):
        b = zig(nz - 1 - k)
        weights = prob[b] * mine
        ds = (weights * (dprob[b] - all_dots)).astype(BF16)
        ds_short[b] = ds
        grad_k = mm(ds, pooled_all)
        grad_v = mm(weights.astype(BF16), short_all)
        kgr_send[b] = (grad_k * gain_both + grad_v).astype(BF16)

        @pl.when(k < nz - 1)
        def _():
            send_key(b).start()

        return gain_sum + (grad_k * kz[b].astype(F32)).sum(axis=0, keepdims=True)

    gain_short = lax.fori_loop(0, nz, second_pass, jnp.zeros((1, HD), F32))
    grad_q = mm_tn(ds_short[...].reshape(nz * span, wide), kz[...].reshape(nz * span, HD)) * gain_both
    qgr_send[...] = grad_q.astype(BF16).reshape(nx, span, HD)
    others_x(lambda o: send_query(o).start())
    qgr_recv[x] = qgr_send[x]
    kgr_recv[z] = kgr_send[z]
    drains.append(lambda: others_x(lambda o: send_query(o).wait_send()))
    drains.append(lambda: others_z(lambda o: send_key(o).wait_send()))
    others_x(lambda o: x_arrived(2, qgr_recv, o))
    others_z(lambda o: z_arrived(1, kgr_recv, o))
    grad_pooled = short_own + qgr_recv[...].astype(F32).sum(axis=0) + kgr_recv[...].astype(F32).sum(axis=0)
    gp_send[...] = grad_pooled.reshape(na, SLOTS, HD)
    others_a(lambda h: exchange(gp_kind, h).start())
    gp_recv[a] = gp_send[a]
    others_a(lambda h: arrived(gp_kind, h))
    drains.append(lambda: others_a(lambda h: exchange(gp_kind, h).wait_send()))
    pass_on = remote(gp_recv, gp_prev, next_send.at[2], next_recv.at[2], following)
    pass_on.start()
    pass_on.wait_recv()
    drains.append(pass_on.wait_send)

    token = iota((T, 16), 0)
    place = iota((T, 16), 1)
    source = jnp.where(token == 0, 15, (token + 15) // 16 - 1)
    spread = jnp.where(place == source, jnp.where(place == SLOTS - 1, not_last, 1.0) * (1.0 / 16), 0.0).astype(BF16)

    def give_back(h):
        return remote(ret_send.at[h], ret_recv.at[h], prev_send.at[h], prev_recv.at[h], previous)

    def scores_back(h):
        cols = columns(h)
        both = ctx[:, cols]
        rows = jnp.concatenate([gp_recv[h], gp_prev[h]], axis=0).astype(BF16)
        grad_mixed = gsrc[pl.ds(0, T), cols].astype(F32) + mm(spread, rows)
        acc[h] = grad_mixed
        incoming = grad_mixed.astype(BF16)
        gm[h] = incoming
        grads = mm_nt(both, incoming)
        grads = jnp.where(prior, grads[:T], grads[T:])
        weights = wt[h]
        dots = (weights * grads).sum(axis=0, keepdims=True)
        ds = weights * (grads - dots)
        ds = jnp.concatenate([jnp.where(prior, ds, 0.0), jnp.where(prior, 0.0, ds)], axis=0).astype(BF16)
        ds_local[h] = ds
        grad_k = mm(ds, both[T:])
        gk_local[h] = grad_k
        gain = (grad_k * both.astype(F32)).sum(axis=0, keepdims=True)
        gr_send[h] = jnp.concatenate([gain, jnp.zeros((7, HD), F32)], axis=0)

        @pl.when(h != a)
        def _():
            exchange(gr_kind, h).start()

        @pl.when(h == a)
        def _():
            gr_recv[h] = gr_send[h]

    grouped(scores_back)
    drains.append(lambda: others_a(lambda h: exchange(gr_kind, h).wait_send()))

    def values_back(h):
        cols = columns(h)
        gain = qg[:, cols] * kg[:, cols] * TEMPER
        to_keys = gk_local[h] * gain + mm(ws[h], gm[h])
        ret_send[h] = to_keys[:T].astype(BF16)
        give_back(h).start()
        acc[h] += mm_tn(ds_local[h], ctx[:, cols]) * gain + to_keys[T:]

    grouped(values_back)
    drains.append(lambda: loop(heads, lambda h: give_back(h).wait_send()))

    others_a(lambda h: arrived(gr_kind, h))
    short_rows = jnp.concatenate([jnp.zeros((1, HD), F32), gain_short, jnp.zeros((6, HD), F32)], axis=0)
    gx[x] = gr_recv[...].sum(axis=0) + short_rows

    def sum_x(other):
        return remote(gx.at[x], gx.at[x], x_send.at[3, other], x_recv.at[3, x], at_x(other))

    def sum_z(other):
        return remote(gz.at[z], gz.at[z], z_send.at[2, other], z_recv.at[2, z], at_z(other))

    def share(other):
        return remote(gfin.at[a], gfin.at[a], a_send.at[3, other], a_recv.at[3, a], at_a(other))

    others_x(lambda o: sum_x(o).start())
    others_x(lambda o: x_arrived(3, gx, o))
    drains.append(lambda: others_x(lambda o: sum_x(o).wait_send()))
    gz[z] = gx[...].sum(axis=0)
    others_z(lambda o: sum_z(o).start())
    others_z(lambda o: z_arrived(2, gz, o))
    drains.append(lambda: others_z(lambda o: sum_z(o).wait_send()))
    gfin[a] = gz[...].sum(axis=0) * (TEMPER * float(total * T) ** (-0.5))
    others_a(lambda h: share(h).start())
    drains.append(lambda: others_a(lambda h: share(h).wait_send()))

    def finish(h):
        give_back(h).wait_recv()
        outv[:, columns(h)] = (acc[h] + ret_recv[h].astype(F32)).astype(BF16)

    grouped(finish)
    store = pltpu.make_async_copy(outv, out, load_sem.at[2])
    store.start()
    drains.append(store.wait)
    others_a(
        lambda h: remote(gfin.at[h], gfin.at[h], a_send.at[3, h], a_recv.at[3, h], at_a(h)).wait_recv()
    )

    def put(h):
        cols = columns(h)
        local, pooled = gfin[h][0:1], gfin[h][1:2]
        rows = [local * kg[:, cols], local * qg[:, cols], pooled * skg[:, cols], pooled * sqg[:, cols]]
        gains[:, cols] = jnp.concatenate(rows, axis=0)

    grouped(put)
    for wait in drains:
        wait()


def shards(sizes, tokens, grad_output, query_gain, key_gain, short_query_gain, short_key_gain):
    nzh, ny, nx, nzl, nc = sizes
    nz, na = nzh * nzl, ny * nc
    width = tokens.shape[1]
    heads = width // HD
    span = na * SLOTS
    vmem = pl.BlockSpec(memory_space=pltpu.VMEM)
    hbm = pl.BlockSpec(memory_space=pl.ANY)
    dma = pltpu.SemaphoreType.DMA
    scratch = [
        pltpu.VMEM((2 * T, width), BF16),
        pltpu.VMEM((T + 16, width), BF16),
        pltpu.VMEM((16, width), BF16),
        pltpu.VMEM((heads, T, HD), BF16),
        pltpu.VMEM((heads, T, HD), BF16),
        pltpu.VMEM((heads, T, T), F32),
        pltpu.VMEM((heads, SLOTS, HD), F32),
        pltpu.VMEM((heads, SLOTS, HD), F32),
        pltpu.VMEM((heads, T, T), F32),
        pltpu.VMEM((heads, 2 * T, T), BF16),
        pltpu.VMEM((na, 16, HD), BF16),
        pltpu.VMEM((na, 16, HD), BF16),
        pltpu.VMEM((nx, 2, span, HD), BF16),
        pltpu.VMEM((nz, span, HD), BF16),
        pltpu.VMEM((nz, span, nx * span), F32),
        pltpu.VMEM((nz, span, nx * span), F32),
        pltpu.VMEM((nz, span, nx * span), BF16),
        pltpu.VMEM((nx, 8, nx * span), F32),
        pltpu.VMEM((nx, span, HD), BF16),
        pltpu.VMEM((nx, span, HD), BF16),
        pltpu.VMEM((nz, span, HD), BF16),
        pltpu.VMEM((nz, span, HD), BF16),
        pltpu.VMEM((na, SLOTS, HD), F32),
        pltpu.VMEM((na, SLOTS, HD), F32),
        pltpu.VMEM((na, SLOTS, HD), F32),
        pltpu.VMEM((heads, T, HD), BF16),
        pltpu.VMEM((heads, 2 * T, T), BF16),
        pltpu.VMEM((heads, 2 * T, HD), F32),
        pltpu.VMEM((heads, T, HD), BF16),
        pltpu.VMEM((heads, T, HD), BF16),
        pltpu.VMEM((heads, T, HD), F32),
        pltpu.VMEM((T, width), BF16),
        pltpu.VMEM((na, 8, HD), F32),
        pltpu.VMEM((na, 8, HD), F32),
        pltpu.VMEM((nx, 8, HD), F32),
        pltpu.VMEM((nz, 8, HD), F32),
        pltpu.VMEM((na, 8, HD), F32),
        dma((3,)),
        dma((3,)),
        dma((3,)),
        dma((heads,)),
        dma((heads,)),
        dma((4, na)),
        dma((4, na)),
        dma((4, nx)),
        dma((4, nx)),
        dma((3, nz)),
        dma((3, nz)),
        dma((heads,)),
        dma((heads,)),
    ]
    return pl.pallas_call(
        functools.partial(kernel, sizes),
        out_shape=(
            jax.ShapeDtypeStruct(tokens.shape, BF16),
            jax.ShapeDtypeStruct((4, width), F32),
        ),
        in_specs=[hbm, hbm, vmem, vmem, vmem, vmem],
        out_specs=(hbm, vmem),
        scratch_shapes=scratch,
        compiler_params=pltpu.CompilerParams(collective_id=0, has_side_effects=True),
        name="hourglass",
    )(
        tokens,
        grad_output,
        query_gain.reshape(1, width),
        key_gain.reshape(1, width),
        short_query_gain.reshape(1, width),
        short_key_gain.reshape(1, width),
    )


def build(mesh, sizes):
    finer = Mesh(mesh.devices.reshape(sizes), AXES)
    return jax.shard_map(
        functools.partial(shards, sizes),
        mesh=finer,
        in_specs=(P(AXES, None), P(AXES, None), P(), P(), P(), P()),
        out_specs=(P(AXES, None), P()),
        check_vma=False,
    )


def solution(mesh):
    return build(mesh, (2, 8, 4, 4, 2))
```

```python
import functools

import jax
import jax.numpy as jnp
from jax import lax
from jax.experimental import pallas as pl
from jax.experimental.pallas import tpu as pltpu
from jax.sharding import Mesh
from jax.sharding import PartitionSpec as P

AXES = ("zh", "y", "x", "zl", "c")
MESH = pl.DeviceIdType.MESH
T = 128
HD = 128
SLOTS = 8
NEGATIVE = -1e30
TEMPER = HD ** (-0.5)
F32 = jnp.float32
BF16 = jnp.bfloat16
GROUP = 8


def mm(a, b):
    return jnp.dot(a, b, preferred_element_type=F32)


def mm_nt(a, b):
    return lax.dot_general(a, b, (((1,), (1,)), ((), ())), preferred_element_type=F32)


def mm_tn(a, b):
    return lax.dot_general(a, b, (((0,), (0,)), ((), ())), preferred_element_type=F32)


def iota(shape, dim):
    return lax.broadcasted_iota(jnp.int32, shape, dim)


def remote(src, dst, send, recv, device):
    return pltpu.make_async_remote_copy(
        src_ref=src, dst_ref=dst, send_sem=send, recv_sem=recv, device_id=device, device_id_type=MESH
    )


def loop(count, body, start=0):
    def step(k, carry):
        body(k)
        return carry

    lax.fori_loop(start, count, step, 0)


def kernel(
    sizes,
    tok, gout, qg, kg, sqg, skg,
    out, gains,
    ctx, gsrc, tnext, qs, ks, own_scores, short, ext, wt, ws, pg_send, pg_recv, pgx, kz, prob, dprob, ds_short, stats,
    qgr_send, qgr_recv, kgr_send, kgr_recv, gp_send, gp_recv, gp_prev,
    gm, ds_local, gk_local, ret_send, ret_recv, acc, outv, gr_send, gr_recv, gx, gz, gfin,
    load_sem, next_send, next_recv, tok_send, tok_recv, a_send, a_recv, x_send, x_recv, z_send, z_recv,
    prev_send, prev_recv,
):
    nzh, ny, nx, nzl, nc = sizes
    nz, na = nzh * nzl, ny * nc
    heads = na
    group = min(GROUP, heads)
    span = na * SLOTS
    zh, y, x, zl, c = [lax.axis_index(name) for name in AXES]
    z = zh * nzl + zl
    a = y * nc + c
    chain = (((zh * ny + y) * nx + x) * nzl + zl) * nc + c
    total = nzh * ny * nx * nzl * nc

    def decode(index):
        return (
            index // (ny * nx * nzl * nc),
            index // (nx * nzl * nc) % ny,
            index // (nzl * nc) % nx,
            index // nc % nzl,
            index % nc,
        )

    following = decode((chain + 1) % total)
    previous = decode((chain + total - 1) % total)

    def at_a(other):
        return (zh, other // nc, x, zl, other % nc)

    def at_x(other):
        return (zh, y, other, zl, c)

    def at_z(other):
        return (other // nzl, y, x, other % nzl, c)

    barrier = pltpu.get_barrier_semaphore()
    drains = []

    def greet(device):
        pl.semaphore_signal(barrier, inc=1, device_id=device, device_id_type=MESH)

    greet(following)
    greet(previous)
    loop(na, lambda k: greet(at_a((a + k) % na)), 1)
    loop(nz, lambda k: greet(at_z((z + k) % nz)), 1)
    loop(nx, lambda k: greet(at_x((x + k) % nx)), 1)

    load_tok = pltpu.make_async_copy(tok, ctx.at[pl.ds(T, T)], load_sem.at[0])
    load_gout = pltpu.make_async_copy(gout, gsrc.at[pl.ds(0, T)], load_sem.at[1])
    load_tok.start()
    load_gout.start()

    pl.semaphore_wait(barrier, 2 + (na - 1) + (nz - 1) + (nx - 1))

    def columns(h):
        return pl.ds(pl.multiple_of(h * HD, HD), HD)

    head_tok = remote(tok.at[pl.ds(0, 16)], tnext, next_send.at[0], next_recv.at[0], previous)
    head_gout = remote(gout.at[pl.ds(0, 16)], gsrc.at[pl.ds(T, 16)], next_send.at[1], next_recv.at[1], previous)
    head_tok.start()
    head_gout.start()
    drains.append(head_tok.wait_send)
    drains.append(head_gout.wait_send)

    def tokens_of(h):
        return remote(
            tok.at[:, columns(h)], ctx.at[pl.ds(0, T), columns(h)], tok_send.at[h], tok_recv.at[h], following
        )

    loop(heads, lambda h: tokens_of(h).start())
    drains.append(lambda: loop(heads, lambda h: tokens_of(h).wait_send()))

    key_row = iota((T, T), 0)
    query_col = iota((T, T), 1)
    prior = key_row > query_col
    first_bias = jnp.where(chain == 0, NEGATIVE, 0.0)
    last_bias = jnp.where(chain == total - 1, NEGATIVE, 0.0)
    not_last = jnp.where(chain == total - 1, 0.0, 1.0)
    self_lane = iota((SLOTS, T), 1) == 0
    slot = iota((SLOTS, T), 0)
    row = iota((SLOTS, T), 1)
    keep = jnp.where(slot == SLOTS - 1, not_last, 1.0)
    pool = jnp.where((row > slot * 16) & (row <= slot * 16 + 16), keep, 0.0).astype(BF16)
    gpool = jnp.where((row >= slot * 16 + 16) & (row < slot * 16 + 32), 1.0, 0.0).astype(BF16)
    tail = iota((SLOTS, HD), 0) == SLOTS - 1

    load_tok.wait()
    load_gout.wait()

    def grouped(body, kind=None):
        def several(g):
            for u in range(group):
                body(g * group + u)
            if kind is not None:
                for u in range(group):
                    dispatch(kind, g * group + u)

        loop(heads // group, several)

    def prepare(h):
        cols = columns(h)
        own_f = ctx[pl.ds(T, T), cols].astype(F32)
        queries = (own_f * qg[:, cols]).astype(BF16)
        keys = (own_f * kg[:, cols]).astype(BF16)
        qs[h] = queries
        ks[h] = keys
        own_scores[h] = mm_nt(keys, queries) * TEMPER
        short[h] = mm(gpool, gsrc[pl.ds(0, T), cols])

    grouped(prepare)
    head_tok.wait_recv()
    head_gout.wait_recv()

    def extend(h):
        cols = columns(h)
        ext_f = tnext[:, cols].astype(F32)[:SLOTS]
        queries = (ext_f * qg[:, cols]).astype(BF16)
        keys = (ext_f * kg[:, cols]).astype(BF16)
        products = queries.astype(F32) * keys.astype(F32)
        same = jnp.broadcast_to(products.sum(axis=1, keepdims=True), (SLOTS, T))
        ext[h] = jnp.where(self_lane, same, mm_nt(queries, ks[h]) + last_bias) * TEMPER
        next_sum = gsrc[pl.ds(T, 16), cols].astype(F32).sum(axis=0, keepdims=True)
        short[h] += jnp.where(tail, next_sum, 0.0)

    def extend_values(h):
        cols = columns(h)
        ext_f = tnext[:, cols].astype(F32)[:SLOTS]
        weights = ext[h]
        found = mm(jnp.where(self_lane, 0.0, weights).astype(BF16), ctx[pl.ds(T, T), cols])
        found = found + weights[:, 0:1] * ext_f
        ext[h] = (ext_f + found).astype(BF16).astype(F32)

    grouped(extend)
    ext_weights = ext[...]
    ext_weights = jnp.exp(ext_weights - ext_weights.max(axis=2, keepdims=True))
    ext_weights = ext_weights * (1.0 / ext_weights.sum(axis=2, keepdims=True))
    ext[...] = ext_weights.astype(BF16).astype(F32)
    grouped(extend_values)

    def exchange(kind, h):
        send, recv, ssem, rsem = kind
        return remote(send.at[h], recv.at[a], ssem.at[h], rsem.at[a], at_a(h))

    def arrived(kind, h):
        send, recv, ssem, rsem = kind
        remote(send.at[h], recv.at[h], ssem.at[h], rsem.at[h], at_a(h)).wait_recv()

    def others_a(body):
        loop(na, lambda k: body((a + k) % na), 1)

    pg_kind = (pg_send, pg_recv, a_send.at[0], a_recv.at[0])
    gp_kind = (gp_send, gp_recv, a_send.at[1], a_recv.at[1])
    gr_kind = (gr_send, gr_recv, a_send.at[2], a_recv.at[2])

    def forward(h):
        cols = columns(h)
        both = ctx[:, cols]
        both_f = both.astype(F32)
        keys = (both_f[:T] * kg[:, cols]).astype(BF16)
        scores = jnp.where(prior, mm_nt(keys, qs[h]) * TEMPER + first_bias, own_scores[h])
        weights = jnp.exp(scores - scores.max(axis=0, keepdims=True))
        weights = weights * (1.0 / weights.sum(axis=0, keepdims=True))
        wt[h] = weights
        split = jnp.concatenate([jnp.where(prior, weights, 0.0), jnp.where(prior, 0.0, weights)], axis=0).astype(BF16)
        ws[h] = split
        mixed = (both_f[T:] + mm_tn(split, both)).astype(BF16)
        pooled = mm(pool, mixed) + jnp.where(tail, ext[h][0:1], 0.0)
        pg_send[h] = jnp.concatenate([pooled * (1.0 / 16), short[h]], axis=0).astype(BF16)

    def dispatch(kind, h):
        @pl.when(h != a)
        def _():
            exchange(kind, h).start()

    def forward_group(g):
        for u in range(group):
            tokens_of(g * group + u).wait_recv()
        for u in range(group):
            forward(g * group + u)
        for u in range(group):
            dispatch(pg_kind, g * group + u)

    loop(heads // group, forward_group)
    pg_recv[a] = pg_send[a]
    others_a(lambda h: arrived(pg_kind, h))
    drains.append(lambda: others_a(lambda h: exchange(pg_kind, h).wait_send()))

    blocks = pg_recv[...].astype(F32)
    pooled_own = blocks[:, :SLOTS].reshape(span, HD).astype(BF16)
    short_own = blocks[:, SLOTS:].reshape(span, HD)
    pgx[x, 0] = pooled_own
    pgx[x, 1] = short_own.astype(BF16)
    kz[z] = pooled_own

    def gather_x(other):
        return remote(pgx.at[x], pgx.at[x], x_send.at[0, other], x_recv.at[0, x], at_x(other))

    def gather_z(other):
        return remote(kz.at[z], kz.at[z], z_send.at[0, other], z_recv.at[0, z], at_z(other))

    def others_x(body):
        loop(nx, lambda k: body((x + k) % nx), 1)

    def others_z(body):
        loop(nz, lambda k: body((z + k) % nz), 1)

    def zig(k):
        half = (k + 1) // 2
        return (z + nz + half * (1 - 2 * ((k + 1) % 2))) % nz

    loop(nz - 1, lambda k: gather_z(zig(nz - 1 - k)).start())
    others_x(lambda o: gather_x(o).start())

    def x_arrived(phase, ref, other):
        remote(ref.at[other], ref.at[other], x_send.at[phase, other], x_recv.at[phase, other], at_x(other)).wait_recv()

    def z_arrived(phase, ref, other):
        remote(ref.at[other], ref.at[other], z_send.at[phase, other], z_recv.at[phase, other], at_z(other)).wait_recv()

    def position(zi, xi, index):
        source, place = index // SLOTS, index % SLOTS
        device = ((zi // nzl * ny + source // nc) * nx + xi) * nzl * nc + zi % nzl * nc + source % nc
        raw = device * SLOTS + place + 1
        return jnp.where(raw == total * SLOTS, 0, raw)

    head_cols = columns(a)
    gain_query = sqg[:, head_cols]
    gain_key = skg[:, head_cols]

    gain_both = gain_query * gain_key * TEMPER
    others_x(lambda o: x_arrived(0, pgx, o))
    wide = nx * span
    pooled_all = pgx[:, 0].reshape(wide, HD)
    short_all = pgx[:, 1].reshape(wide, HD)
    queries_all = (pooled_all.astype(F32) * gain_query).astype(BF16)
    query_index = iota((1, wide), 1)
    query_pos = position(z, query_index // span, query_index % span)
    key_index = iota((span, 1), 0)

    def first_pass(k, highest):
        b = zig(k)

        @pl.when(k > 0)
        def _():
            z_arrived(0, kz, b)

        values = kz[b]
        keys = (values.astype(F32) * gain_key).astype(BF16)
        visible = position(b, x, key_index) <= query_pos
        scores = jnp.where(visible, mm_nt(keys, queries_all) * TEMPER, NEGATIVE)
        prob[b] = scores
        dprob[b] = mm_nt(values, short_all)
        return jnp.maximum(highest, scores.max(axis=0, keepdims=True))

    highest = lax.fori_loop(0, nz, first_pass, jnp.full((1, wide), 0.1 * NEGATIVE, F32))
    drains.append(lambda: others_z(lambda o: gather_z(o).wait_send()))
    drains.append(lambda: others_x(lambda o: gather_x(o).wait_send()))

    def totals(b, carry):
        sums, dots = carry
        weights = jnp.exp(prob[b] - highest)
        prob[b] = weights
        return (
            sums + weights.sum(axis=0, keepdims=True),
            dots + (weights * dprob[b]).sum(axis=0, keepdims=True),
        )

    zero = jnp.zeros((1, wide), F32)
    sums, dots = lax.fori_loop(0, nz, totals, (zero, zero))
    stats[x] = jnp.concatenate([highest, sums, dots, jnp.zeros((5, wide), F32)], axis=0)

    def send_stats(other):
        return remote(stats.at[x], stats.at[x], x_send.at[1, other], x_recv.at[1, x], at_x(other))

    others_x(lambda o: send_stats(o).start())
    others_x(lambda o: x_arrived(1, stats, o))
    drains.append(lambda: others_x(lambda o: send_stats(o).wait_send()))

    def send_query(other):
        return remote(qgr_send.at[other], qgr_recv.at[x], x_send.at[2, other], x_recv.at[2, x], at_x(other))

    def send_key(other):
        return remote(kgr_send.at[other], kgr_recv.at[z], z_send.at[1, other], z_recv.at[1, z], at_z(other))

    pieces = [stats[s] for s in range(nx)]
    top = pieces[0][0:1]
    for piece in pieces[1:]:
        top = jnp.maximum(top, piece[0:1])
    all_sums = jnp.zeros((1, wide), F32)
    all_dots = jnp.zeros((1, wide), F32)
    for piece in pieces:
        factor = jnp.exp(piece[0:1] - top)
        all_sums = all_sums + piece[1:2] * factor
        all_dots = all_dots + piece[2:3] * factor
    inverse = 1.0 / all_sums
    mine = jnp.exp(highest - top) * inverse
    all_dots = all_dots * inverse

    def second_pass(k, gain_sum):
        b = zig(nz - 1 - k)
        weights = prob[b] * mine
        ds = (weights * (dprob[b] - all_dots)).astype(BF16)
        ds_short[b] = ds
        grad_k = mm(ds, pooled_all)
        grad_v = mm(weights.astype(BF16), short_all)
        kgr_send[b] = (grad_k * gain_both + grad_v).astype(BF16)

        @pl.when(k < nz - 1)
        def _():
            send_key(b).start()

        return gain_sum + (grad_k * kz[b].astype(F32)).sum(axis=0, keepdims=True)

    gain_short = lax.fori_loop(0, nz, second_pass, jnp.zeros((1, HD), F32))
    grad_q = mm_tn(ds_short[...].reshape(nz * span, wide), kz[...].reshape(nz * span, HD)) * gain_both
    qgr_send[...] = grad_q.astype(BF16).reshape(nx, span, HD)
    others_x(lambda o: send_query(o).start())
    qgr_recv[x] = qgr_send[x]
    kgr_recv[z] = kgr_send[z]
    drains.append(lambda: others_x(lambda o: send_query(o).wait_send()))
    drains.append(lambda: others_z(lambda o: send_key(o).wait_send()))
    others_x(lambda o: x_arrived(2, qgr_recv, o))
    others_z(lambda o: z_arrived(1, kgr_recv, o))
    grad_pooled = short_own + qgr_recv[...].astype(F32).sum(axis=0) + kgr_recv[...].astype(F32).sum(axis=0)
    gp_send[...] = grad_pooled.reshape(na, SLOTS, HD)
    others_a(lambda h: exchange(gp_kind, h).start())
    gp_recv[a] = gp_send[a]
    others_a(lambda h: arrived(gp_kind, h))
    drains.append(lambda: others_a(lambda h: exchange(gp_kind, h).wait_send()))
    pass_on = remote(gp_recv, gp_prev, next_send.at[2], next_recv.at[2], following)
    pass_on.start()
    pass_on.wait_recv()
    drains.append(pass_on.wait_send)

    token = iota((T, 16), 0)
    place = iota((T, 16), 1)
    source = jnp.where(token == 0, 15, (token + 15) // 16 - 1)
    spread = jnp.where(place == source, jnp.where(place == SLOTS - 1, not_last, 1.0) * (1.0 / 16), 0.0).astype(BF16)

    def give_back(h):
        return remote(ret_send.at[h], ret_recv.at[h], prev_send.at[h], prev_recv.at[h], previous)

    def scores_back(h):
        cols = columns(h)
        both = ctx[:, cols]
        rows = jnp.concatenate([gp_recv[h], gp_prev[h]], axis=0).astype(BF16)
        grad_mixed = gsrc[pl.ds(0, T), cols].astype(F32) + mm(spread, rows)
        acc[h] = grad_mixed
        incoming = grad_mixed.astype(BF16)
        gm[h] = incoming
        grads = mm_nt(both, incoming)
        grads = jnp.where(prior, grads[:T], grads[T:])
        weights = wt[h]
        dots = (weights * grads).sum(axis=0, keepdims=True)
        ds = weights * (grads - dots)
        ds = jnp.concatenate([jnp.where(prior, ds, 0.0), jnp.where(prior, 0.0, ds)], axis=0).astype(BF16)
        ds_local[h] = ds
        grad_k = mm(ds, both[T:])
        gk_local[h] = grad_k
        gain = (grad_k * both.astype(F32)).sum(axis=0, keepdims=True)
        gr_send[h] = jnp.concatenate([gain, jnp.zeros((7, HD), F32)], axis=0)

    grouped(scores_back, gr_kind)
    gr_recv[a] = gr_send[a]
    drains.append(lambda: others_a(lambda h: exchange(gr_kind, h).wait_send()))

    def values_back(h):
        cols = columns(h)
        gain = qg[:, cols] * kg[:, cols] * TEMPER
        to_keys = gk_local[h] * gain + mm(ws[h], gm[h])
        ret_send[h] = to_keys[:T].astype(BF16)
        acc[h] += mm_tn(ds_local[h], ctx[:, cols]) * gain + to_keys[T:]

    def values_group(g):
        for u in range(group):
            values_back(g * group + u)
        for u in range(group):
            give_back(g * group + u).start()

    loop(heads // group, values_group)
    drains.append(lambda: loop(heads, lambda h: give_back(h).wait_send()))

    others_a(lambda h: arrived(gr_kind, h))
    short_rows = jnp.concatenate([jnp.zeros((1, HD), F32), gain_short, jnp.zeros((6, HD), F32)], axis=0)
    gx[x] = gr_recv[...].sum(axis=0) + short_rows

    def sum_x(other):
        return remote(gx.at[x], gx.at[x], x_send.at[3, other], x_recv.at[3, x], at_x(other))

    def sum_z(other):
        return remote(gz.at[z], gz.at[z], z_send.at[2, other], z_recv.at[2, z], at_z(other))

    def share(other):
        return remote(gfin.at[a], gfin.at[a], a_send.at[3, other], a_recv.at[3, a], at_a(other))

    others_x(lambda o: sum_x(o).start())
    others_x(lambda o: x_arrived(3, gx, o))
    drains.append(lambda: others_x(lambda o: sum_x(o).wait_send()))
    gz[z] = gx[...].sum(axis=0)
    others_z(lambda o: sum_z(o).start())
    others_z(lambda o: z_arrived(2, gz, o))
    drains.append(lambda: others_z(lambda o: sum_z(o).wait_send()))
    gfin[a] = gz[...].sum(axis=0) * (TEMPER * float(total * T) ** (-0.5))
    others_a(lambda h: share(h).start())
    drains.append(lambda: others_a(lambda h: share(h).wait_send()))

    def finish(h):
        give_back(h).wait_recv()
        outv[:, columns(h)] = (acc[h] + ret_recv[h].astype(F32)).astype(BF16)

    grouped(finish)
    store = pltpu.make_async_copy(outv, out, load_sem.at[2])
    store.start()
    drains.append(store.wait)
    others_a(
        lambda h: remote(gfin.at[h], gfin.at[h], a_send.at[3, h], a_recv.at[3, h], at_a(h)).wait_recv()
    )

    def put(h):
        cols = columns(h)
        local, pooled = gfin[h][0:1], gfin[h][1:2]
        rows = [local * kg[:, cols], local * qg[:, cols], pooled * skg[:, cols], pooled * sqg[:, cols]]
        gains[:, cols] = jnp.concatenate(rows, axis=0)

    grouped(put)
    for wait in drains:
        wait()


def shards(sizes, tokens, grad_output, query_gain, key_gain, short_query_gain, short_key_gain):
    nzh, ny, nx, nzl, nc = sizes
    nz, na = nzh * nzl, ny * nc
    width = tokens.shape[1]
    heads = width // HD
    span = na * SLOTS
    vmem = pl.BlockSpec(memory_space=pltpu.VMEM)
    hbm = pl.BlockSpec(memory_space=pl.ANY)
    dma = pltpu.SemaphoreType.DMA
    scratch = [
        pltpu.VMEM((2 * T, width), BF16),
        pltpu.VMEM((T + 16, width), BF16),
        pltpu.VMEM((16, width), BF16),
        pltpu.VMEM((heads, T, HD), BF16),
        pltpu.VMEM((heads, T, HD), BF16),
        pltpu.VMEM((heads, T, T), F32),
        pltpu.VMEM((heads, SLOTS, HD), F32),
        pltpu.VMEM((heads, SLOTS, HD), F32),
        pltpu.VMEM((heads, T, T), F32),
        pltpu.VMEM((heads, 2 * T, T), BF16),
        pltpu.VMEM((na, 16, HD), BF16),
        pltpu.VMEM((na, 16, HD), BF16),
        pltpu.VMEM((nx, 2, span, HD), BF16),
        pltpu.VMEM((nz, span, HD), BF16),
        pltpu.VMEM((nz, span, nx * span), F32),
        pltpu.VMEM((nz, span, nx * span), F32),
        pltpu.VMEM((nz, span, nx * span), BF16),
        pltpu.VMEM((nx, 8, nx * span), F32),
        pltpu.VMEM((nx, span, HD), BF16),
        pltpu.VMEM((nx, span, HD), BF16),
        pltpu.VMEM((nz, span, HD), BF16),
        pltpu.VMEM((nz, span, HD), BF16),
        pltpu.VMEM((na, SLOTS, HD), F32),
        pltpu.VMEM((na, SLOTS, HD), F32),
        pltpu.VMEM((na, SLOTS, HD), F32),
        pltpu.VMEM((heads, T, HD), BF16),
        pltpu.VMEM((heads, 2 * T, T), BF16),
        pltpu.VMEM((heads, 2 * T, HD), F32),
        pltpu.VMEM((heads, T, HD), BF16),
        pltpu.VMEM((heads, T, HD), BF16),
        pltpu.VMEM((heads, T, HD), F32),
        pltpu.VMEM((T, width), BF16),
        pltpu.VMEM((na, 8, HD), F32),
        pltpu.VMEM((na, 8, HD), F32),
        pltpu.VMEM((nx, 8, HD), F32),
        pltpu.VMEM((nz, 8, HD), F32),
        pltpu.VMEM((na, 8, HD), F32),
        dma((3,)),
        dma((3,)),
        dma((3,)),
        dma((heads,)),
        dma((heads,)),
        dma((4, na)),
        dma((4, na)),
        dma((4, nx)),
        dma((4, nx)),
        dma((3, nz)),
        dma((3, nz)),
        dma((heads,)),
        dma((heads,)),
    ]
    return pl.pallas_call(
        functools.partial(kernel, sizes),
        out_shape=(
            jax.ShapeDtypeStruct(tokens.shape, BF16),
            jax.ShapeDtypeStruct((4, width), F32),
        ),
        in_specs=[hbm, hbm, vmem, vmem, vmem, vmem],
        out_specs=(hbm, vmem),
        scratch_shapes=scratch,
        compiler_params=pltpu.CompilerParams(collective_id=0, has_side_effects=True),
        name="hourglass",
    )(
        tokens,
        grad_output,
        query_gain.reshape(1, width),
        key_gain.reshape(1, width),
        short_query_gain.reshape(1, width),
        short_key_gain.reshape(1, width),
    )


def build(mesh, sizes):
    finer = Mesh(mesh.devices.reshape(sizes), AXES)
    return jax.shard_map(
        functools.partial(shards, sizes),
        mesh=finer,
        in_specs=(P(AXES, None), P(AXES, None), P(), P(), P(), P()),
        out_specs=(P(AXES, None), P()),
        check_vma=False,
    )


def solution(mesh):
    return build(mesh, (2, 8, 4, 4, 2))
```

```python
import functools

import jax
import jax.numpy as jnp
from jax import lax
from jax.experimental import pallas as pl
from jax.experimental.pallas import tpu as pltpu
from jax.sharding import Mesh
from jax.sharding import PartitionSpec as P

AXES = ("zh", "y", "x", "zl", "c")
MESH = pl.DeviceIdType.MESH
T = 128
HD = 128
SLOTS = 8
NEGATIVE = -1e30
TEMPER = HD ** (-0.5)
F32 = jnp.float32
BF16 = jnp.bfloat16
GROUP = 8


def mm(a, b):
    return jnp.dot(a, b, preferred_element_type=F32)


def mm_nt(a, b):
    return lax.dot_general(a, b, (((1,), (1,)), ((), ())), preferred_element_type=F32)


def mm_tn(a, b):
    return lax.dot_general(a, b, (((0,), (0,)), ((), ())), preferred_element_type=F32)


def iota(shape, dim):
    return lax.broadcasted_iota(jnp.int32, shape, dim)


def remote(src, dst, send, recv, device):
    return pltpu.make_async_remote_copy(
        src_ref=src, dst_ref=dst, send_sem=send, recv_sem=recv, device_id=device, device_id_type=MESH
    )


def loop(count, body, start=0):
    def step(k, carry):
        body(k)
        return carry

    lax.fori_loop(start, count, step, 0)


def kernel(
    sizes,
    tok, gout, qg, kg, sqg, skg,
    out, gains,
    ctx, gsrc, tnext, qs, ks, own_scores, short, ext, wt, ws, pg_send, pg_recv, pgx, kz, prob, dprob, ds_short, stats,
    qgr_send, qgr_recv, kgr_send, kgr_recv, gp_send, gp_recv, gp_prev,
    gm, ds_local, gk_local, ret_send, ret_recv, acc, outv, gsum, gpart, gx, gy, gz, gfin,
    load_sem, next_send, next_recv, tok_send, tok_recv, a_send, a_recv, x_send, x_recv, z_send, z_recv,
    prev_send, prev_recv, c_send, c_recv, y_send, y_recv,
):
    nzh, ny, nx, nzl, nc = sizes
    nz, na = nzh * nzl, ny * nc
    heads = na
    group = min(GROUP, heads)
    half = heads // 2
    stride = min(4, heads)
    span = na * SLOTS
    zh, y, x, zl, c = [lax.axis_index(name) for name in AXES]
    z = zh * nzl + zl
    a = y * nc + c
    chain = (((zh * ny + y) * nx + x) * nzl + zl) * nc + c
    total = nzh * ny * nx * nzl * nc

    def decode(index):
        return (
            index // (ny * nx * nzl * nc),
            index // (nx * nzl * nc) % ny,
            index // (nzl * nc) % nx,
            index // nc % nzl,
            index % nc,
        )

    following = decode((chain + 1) % total)
    previous = decode((chain + total - 1) % total)

    def at_a(other):
        return (zh, other // nc, x, zl, other % nc)

    def at_x(other):
        return (zh, y, other, zl, c)

    def at_z(other):
        return (other // nzl, y, x, other % nzl, c)

    barrier = pltpu.get_barrier_semaphore()
    drains = []

    def greet(device):
        pl.semaphore_signal(barrier, inc=1, device_id=device, device_id_type=MESH)

    greet(following)
    greet(previous)
    loop(na, lambda k: greet(at_a((a + k) % na)), 1)
    loop(nz, lambda k: greet(at_z((z + k) % nz)), 1)
    loop(nx, lambda k: greet(at_x((x + k) % nx)), 1)

    load_tok = pltpu.make_async_copy(tok, ctx.at[pl.ds(T, T)], load_sem.at[0])
    load_gout = pltpu.make_async_copy(gout, gsrc.at[pl.ds(0, T)], load_sem.at[1])
    load_tok.start()
    load_gout.start()

    pl.semaphore_wait(barrier, 2 + (na - 1) + (nz - 1) + (nx - 1))

    def columns(h):
        return pl.ds(pl.multiple_of(h * HD, HD), HD)

    head_tok = remote(tok.at[pl.ds(0, 16)], tnext, next_send.at[0], next_recv.at[0], previous)
    head_gout = remote(gout.at[pl.ds(0, 16)], gsrc.at[pl.ds(T, 16)], next_send.at[1], next_recv.at[1], previous)
    head_tok.start()
    head_gout.start()
    drains.append(head_tok.wait_send)
    drains.append(head_gout.wait_send)

    def tokens_of(h):
        return remote(
            tok.at[:, columns(h)], ctx.at[pl.ds(0, T), columns(h)], tok_send.at[h], tok_recv.at[h], following
        )

    loop(heads, lambda h: tokens_of(h).start())
    drains.append(lambda: loop(heads, lambda h: tokens_of(h).wait_send()))

    key_row = iota((T, T), 0)
    query_col = iota((T, T), 1)
    prior = key_row > query_col
    first_bias = jnp.where(chain == 0, NEGATIVE, 0.0)
    last_bias = jnp.where(chain == total - 1, NEGATIVE, 0.0)
    not_last = jnp.where(chain == total - 1, 0.0, 1.0)
    self_lane = iota((SLOTS, T), 1) == 0
    slot = iota((SLOTS, T), 0)
    row = iota((SLOTS, T), 1)
    keep = jnp.where(slot == SLOTS - 1, not_last, 1.0)
    pool = jnp.where((row > slot * 16) & (row <= slot * 16 + 16), keep, 0.0).astype(BF16)
    gpool = jnp.where((row >= slot * 16 + 16) & (row < slot * 16 + 32), 1.0, 0.0).astype(BF16)
    tail = iota((SLOTS, HD), 0) == SLOTS - 1

    load_tok.wait()
    load_gout.wait()

    def grouped(body):
        def several(g):
            for u in range(group):
                body(g * group + u)

        loop(heads // group, several)

    def prepare(h):
        cols = columns(h)
        own_f = ctx[pl.ds(T, T), cols].astype(F32)
        queries = (own_f * qg[:, cols]).astype(BF16)
        keys = (own_f * kg[:, cols]).astype(BF16)
        qs[h] = queries
        ks[h] = keys
        own_scores[h] = mm_nt(keys, queries) * TEMPER
        short[h] = mm(gpool, gsrc[pl.ds(0, T), cols])

    grouped(prepare)
    head_tok.wait_recv()
    head_gout.wait_recv()

    def extend(h):
        cols = columns(h)
        ext_f = tnext[:, cols].astype(F32)[:SLOTS]
        queries = (ext_f * qg[:, cols]).astype(BF16)
        keys = (ext_f * kg[:, cols]).astype(BF16)
        products = queries.astype(F32) * keys.astype(F32)
        same = jnp.broadcast_to(products.sum(axis=1, keepdims=True), (SLOTS, T))
        ext[h] = jnp.where(self_lane, same, mm_nt(queries, ks[h]) + last_bias) * TEMPER
        next_sum = gsrc[pl.ds(T, 16), cols].astype(F32).sum(axis=0, keepdims=True)
        short[h] += jnp.where(tail, next_sum, 0.0)

    def extend_values(h):
        cols = columns(h)
        ext_f = tnext[:, cols].astype(F32)[:SLOTS]
        weights = ext[h]
        found = mm(jnp.where(self_lane, 0.0, weights).astype(BF16), ctx[pl.ds(T, T), cols])
        found = found + weights[:, 0:1] * ext_f
        ext[h] = (ext_f + found).astype(BF16).astype(F32)

    grouped(extend)
    ext_weights = ext[...]
    ext_weights = jnp.exp(ext_weights - ext_weights.max(axis=2, keepdims=True))
    ext_weights = ext_weights * (1.0 / ext_weights.sum(axis=2, keepdims=True))
    ext[...] = ext_weights.astype(BF16).astype(F32)
    grouped(extend_values)

    def exchange(kind, h):
        send, recv, ssem, rsem = kind
        return remote(send.at[h], recv.at[a], ssem.at[h], rsem.at[a], at_a(h))

    def arrived(kind, h):
        send, recv, ssem, rsem = kind
        remote(send.at[h], recv.at[h], ssem.at[h], rsem.at[h], at_a(h)).wait_recv()

    def others_a(body):
        loop(na, lambda k: body((a + k) % na), 1)

    pg_kind = (pg_send, pg_recv, a_send.at[0], a_recv.at[0])
    gp_kind = (gp_send, gp_recv, a_send.at[1], a_recv.at[1])

    def forward(h):
        cols = columns(h)
        both = ctx[:, cols]
        both_f = both.astype(F32)
        keys = (both_f[:T] * kg[:, cols]).astype(BF16)
        scores = jnp.where(prior, mm_nt(keys, qs[h]) * TEMPER + first_bias, own_scores[h])
        weights = jnp.exp(scores - scores.max(axis=0, keepdims=True))
        weights = weights * (1.0 / weights.sum(axis=0, keepdims=True))
        wt[h] = weights
        split = jnp.concatenate([jnp.where(prior, weights, 0.0), jnp.where(prior, 0.0, weights)], axis=0).astype(BF16)
        ws[h] = split
        mixed = (both_f[T:] + mm_tn(split, both)).astype(BF16)
        pooled = mm(pool, mixed) + jnp.where(tail, ext[h][0:1], 0.0)
        pg_send[h] = jnp.concatenate([pooled * (1.0 / 16), short[h]], axis=0).astype(BF16)

    def dispatch(kind, h):
        @pl.when(h != a)
        def _():
            exchange(kind, h).start()

    def forward_group(g):
        for u in range(stride):
            tokens_of(g * stride + u).wait_recv()
        for u in range(stride):
            forward(g * stride + u)
        for u in range(stride):
            dispatch(pg_kind, g * stride + u)

    loop(heads // stride, forward_group)
    pg_recv[a] = pg_send[a]
    others_a(lambda h: arrived(pg_kind, h))
    drains.append(lambda: others_a(lambda h: exchange(pg_kind, h).wait_send()))

    blocks = pg_recv[...].astype(F32)
    pooled_own = blocks[:, :SLOTS].reshape(span, HD).astype(BF16)
    short_own = blocks[:, SLOTS:].reshape(span, HD)
    pgx[x, 0] = pooled_own
    pgx[x, 1] = short_own.astype(BF16)
    kz[z] = pooled_own

    def gather_x(other):
        return remote(pgx.at[x], pgx.at[x], x_send.at[0, other], x_recv.at[0, x], at_x(other))

    def gather_z(other):
        return remote(kz.at[z], kz.at[z], z_send.at[0, other], z_recv.at[0, z], at_z(other))

    def others_x(body):
        loop(nx, lambda k: body((x + k) % nx), 1)

    def others_z(body):
        loop(nz, lambda k: body((z + k) % nz), 1)

    def zig(k):
        half = (k + 1) // 2
        return (z + nz + half * (1 - 2 * ((k + 1) % 2))) % nz

    loop(nz - 1, lambda k: gather_z(zig(nz - 1 - k)).start())
    others_x(lambda o: gather_x(o).start())

    def x_arrived(phase, ref, other):
        remote(ref.at[other], ref.at[other], x_send.at[phase, other], x_recv.at[phase, other], at_x(other)).wait_recv()

    def z_arrived(phase, ref, other):
        remote(ref.at[other], ref.at[other], z_send.at[phase, other], z_recv.at[phase, other], at_z(other)).wait_recv()

    def position(zi, xi, index):
        source, place = index // SLOTS, index % SLOTS
        device = ((zi // nzl * ny + source // nc) * nx + xi) * nzl * nc + zi % nzl * nc + source % nc
        raw = device * SLOTS + place + 1
        return jnp.where(raw == total * SLOTS, 0, raw)

    head_cols = columns(a)
    gain_query = sqg[:, head_cols]
    gain_key = skg[:, head_cols]

    gain_both = gain_query * gain_key * TEMPER
    others_x(lambda o: x_arrived(0, pgx, o))
    wide = nx * span
    pooled_all = pgx[:, 0].reshape(wide, HD)
    short_all = pgx[:, 1].reshape(wide, HD)
    queries_all = (pooled_all.astype(F32) * gain_query).astype(BF16)
    query_index = iota((1, wide), 1)
    query_pos = position(z, query_index // span, query_index % span)
    key_index = iota((span, 1), 0)

    def first_pass(k, highest):
        b = zig(k)

        @pl.when(k > 0)
        def _():
            z_arrived(0, kz, b)

        values = kz[b]
        keys = (values.astype(F32) * gain_key).astype(BF16)
        visible = position(b, x, key_index) <= query_pos
        scores = jnp.where(visible, mm_nt(keys, queries_all) * TEMPER, NEGATIVE)
        prob[b] = scores
        dprob[b] = mm_nt(values, short_all)
        return jnp.maximum(highest, scores.max(axis=0, keepdims=True))

    highest = lax.fori_loop(0, nz, first_pass, jnp.full((1, wide), 0.1 * NEGATIVE, F32))
    drains.append(lambda: others_z(lambda o: gather_z(o).wait_send()))
    drains.append(lambda: others_x(lambda o: gather_x(o).wait_send()))

    def totals(k, carry):
        sums, dots = carry
        for b in (2 * k, 2 * k + 1):
            weights = jnp.exp(prob[b] - highest)
            prob[b] = weights
            sums = sums + weights.sum(axis=0, keepdims=True)
            dots = dots + (weights * dprob[b]).sum(axis=0, keepdims=True)
        return sums, dots

    zero = jnp.zeros((1, wide), F32)
    sums, dots = lax.fori_loop(0, nz // 2, totals, (zero, zero))
    stats[x] = jnp.concatenate([highest, sums, dots, jnp.zeros((1, wide), F32)], axis=0)

    def send_stats(other):
        return remote(stats.at[x], stats.at[x], x_send.at[1, other], x_recv.at[1, x], at_x(other))

    others_x(lambda o: send_stats(o).start())
    others_x(lambda o: x_arrived(1, stats, o))
    drains.append(lambda: others_x(lambda o: send_stats(o).wait_send()))

    def send_query(other):
        return remote(qgr_send.at[other], qgr_recv.at[x], x_send.at[2, other], x_recv.at[2, x], at_x(other))

    def send_key(other):
        return remote(kgr_send.at[other], kgr_recv.at[z], z_send.at[1, other], z_recv.at[1, z], at_z(other))

    pieces = [stats[s] for s in range(nx)]
    top = pieces[0][0:1]
    for piece in pieces[1:]:
        top = jnp.maximum(top, piece[0:1])
    all_sums = jnp.zeros((1, wide), F32)
    all_dots = jnp.zeros((1, wide), F32)
    for piece in pieces:
        factor = jnp.exp(piece[0:1] - top)
        all_sums = all_sums + piece[1:2] * factor
        all_dots = all_dots + piece[2:3] * factor
    inverse = 1.0 / all_sums
    mine = jnp.exp(highest - top) * inverse
    all_dots = all_dots * inverse

    def second_pass(k, gain_sum):
        for u in range(2):
            b = zig(nz - 1 - 2 * k - u)
            weights = prob[b] * mine
            ds = (weights * (dprob[b] - all_dots)).astype(BF16)
            ds_short[b] = ds
            grad_k = mm(ds, pooled_all)
            grad_v = mm(weights.astype(BF16), short_all)
            kgr_send[b] = (grad_k * gain_both + grad_v).astype(BF16)
            gain_sum = gain_sum + (grad_k * kz[b].astype(F32)).sum(axis=0, keepdims=True)
        send_key(zig(nz - 1 - 2 * k)).start()

        @pl.when(2 * k + 1 < nz - 1)
        def _():
            send_key(zig(nz - 2 - 2 * k)).start()

        return gain_sum

    gain_short = lax.fori_loop(0, nz // 2, second_pass, jnp.zeros((1, HD), F32))
    gsum[...] = jnp.zeros_like(gsum)
    gsum[a // half, pl.ds(half + a % half, 1), :] = gain_short
    grad_q = mm_tn(ds_short[...].reshape(nz * span, wide), kz[...].reshape(nz * span, HD)) * gain_both
    qgr_send[...] = grad_q.astype(BF16).reshape(nx, span, HD)
    others_x(lambda o: send_query(o).start())
    qgr_recv[x] = qgr_send[x]
    kgr_recv[z] = kgr_send[z]
    drains.append(lambda: others_x(lambda o: send_query(o).wait_send()))
    drains.append(lambda: others_z(lambda o: send_key(o).wait_send()))
    others_x(lambda o: x_arrived(2, qgr_recv, o))
    others_z(lambda o: z_arrived(1, kgr_recv, o))
    grad_pooled = short_own + qgr_recv[...].astype(F32).sum(axis=0) + kgr_recv[...].astype(F32).sum(axis=0)
    gp_send[...] = grad_pooled.reshape(na, SLOTS, HD)
    others_a(lambda h: exchange(gp_kind, h).start())
    gp_recv[a] = gp_send[a]
    others_a(lambda h: arrived(gp_kind, h))
    drains.append(lambda: others_a(lambda h: exchange(gp_kind, h).wait_send()))
    pass_on = remote(gp_recv, gp_prev, next_send.at[2], next_recv.at[2], following)
    pass_on.start()
    pass_on.wait_recv()
    drains.append(pass_on.wait_send)

    token = iota((T, 16), 0)
    place = iota((T, 16), 1)
    source = jnp.where(token == 0, 15, (token + 15) // 16 - 1)
    spread = jnp.where(place == source, jnp.where(place == SLOTS - 1, not_last, 1.0) * (1.0 / 16), 0.0).astype(BF16)

    def give_back(h):
        return remote(ret_send.at[h], ret_recv.at[h], prev_send.at[h], prev_recv.at[h], previous)

    def scores_back(h):
        cols = columns(h)
        both = ctx[:, cols]
        rows = jnp.concatenate([gp_recv[h], gp_prev[h]], axis=0).astype(BF16)
        grad_mixed = gsrc[pl.ds(0, T), cols].astype(F32) + mm(spread, rows)
        acc[h] = grad_mixed
        incoming = grad_mixed.astype(BF16)
        gm[h] = incoming
        grads = mm_nt(both, incoming)
        grads = jnp.where(prior, grads[:T], grads[T:])
        weights = wt[h]
        dots = (weights * grads).sum(axis=0, keepdims=True)
        ds = weights * (grads - dots)
        ds = jnp.concatenate([jnp.where(prior, ds, 0.0), jnp.where(prior, 0.0, ds)], axis=0).astype(BF16)
        ds_local[h] = ds
        grad_k = mm(ds, both[T:])
        gk_local[h] = grad_k
        gain = (grad_k * both.astype(F32)).sum(axis=0, keepdims=True)
        gsum[h // half, pl.ds(h % half, 1), :] = gain

    partner = (zh, y, x, zl, 1 - c)

    def at_y(other):
        return (zh, other, x, zl, c)

    def others_y(body):
        loop(ny, lambda k: body((y + k) % ny), 1)

    halve = remote(gsum.at[1 - c], gpart, c_send.at[0], c_recv.at[0], partner)
    share = remote(gfin.at[c], gfin.at[c], c_send.at[1], c_recv.at[1], partner)

    def sum_z(other):
        return remote(gz.at[z], gz.at[z], z_send.at[2, other], z_recv.at[2, z], at_z(other))

    def sum_x(other):
        return remote(gx.at[x], gx.at[x], x_send.at[3, other], x_recv.at[3, x], at_x(other))

    def sum_y(other):
        return remote(gy.at[y], gy.at[y], y_send.at[other], y_recv.at[y], at_y(other))


    def values_back(h):
        cols = columns(h)
        gain = qg[:, cols] * kg[:, cols] * TEMPER
        to_keys = gk_local[h] * gain + mm(ws[h], gm[h])
        ret_send[h] = to_keys[:T].astype(BF16)
        acc[h] += mm_tn(ds_local[h], ctx[:, cols]) * gain + to_keys[T:]

    def values_group(g):
        for u in range(group):
            values_back(g * group + u)
        for u in range(group):
            give_back(g * group + u).start()

    grouped(scores_back)
    halve.start()
    values_group(0)
    halve.wait_recv()
    gy[y] = (gsum[c] + gpart[...]).astype(BF16)
    others_y(lambda o: sum_y(o).start())
    loop(heads // group, values_group, 1)
    drains.append(halve.wait_send)
    drains.append(lambda: loop(heads, lambda h: give_back(h).wait_send()))
    drains.append(lambda: others_y(lambda o: sum_y(o).wait_send()))

    others_y(lambda o: remote(gy.at[o], gy.at[o], y_send.at[o], y_recv.at[o], at_y(o)).wait_recv())
    gx[x] = gy[...].astype(F32).sum(axis=0).astype(BF16)
    others_x(lambda o: sum_x(o).start())
    others_x(lambda o: x_arrived(3, gx, o))
    drains.append(lambda: others_x(lambda o: sum_x(o).wait_send()))
    gz[z] = gx[...].astype(F32).sum(axis=0).astype(BF16)
    others_z(lambda o: sum_z(o).start())
    others_z(lambda o: z_arrived(2, gz, o))
    drains.append(lambda: others_z(lambda o: sum_z(o).wait_send()))
    gfin[c] = gz[...].astype(F32).sum(axis=0) * (TEMPER * float(total * T) ** (-0.5))
    share.start()
    drains.append(share.wait_send)

    def finish(h):
        give_back(h).wait_recv()
        outv[:, columns(h)] = (acc[h] + ret_recv[h].astype(F32)).astype(BF16)

    grouped(finish)
    store = pltpu.make_async_copy(outv, out, load_sem.at[2])
    store.start()
    drains.append(store.wait)
    remote(gfin.at[1 - c], gfin.at[1 - c], c_send.at[1], c_recv.at[1], partner).wait_recv()
    for side in range(2):
        rows = gfin[side]
        for r in range(half):
            cols = pl.ds((side * half + r) * HD, HD)
            local, pooled = rows[r : r + 1], rows[half + r : half + r + 1]
            gains[:, cols] = jnp.concatenate(
                [local * kg[:, cols], local * qg[:, cols], pooled * skg[:, cols], pooled * sqg[:, cols]], axis=0
            )

    for wait in drains:
        wait()


def relay(first, second, out, gains, hold, small, arrive, leave):
    rows = hold.shape[0] // 4
    pairs = [(first.at[pl.ds(k * rows, rows)], hold.at[pl.ds(k * rows, rows)], out.at[pl.ds(k * rows, rows)]) for k in range(4)]
    pairs.append((second, small, gains))
    fetch = [pltpu.make_async_copy(i, m, arrive.at[k]) for k, (i, m, o) in enumerate(pairs)]
    store = [pltpu.make_async_copy(m, o, leave.at[k]) for k, (i, m, o) in enumerate(pairs)]
    for copy in fetch:
        copy.start()
    for k in range(5):
        fetch[k].wait()
        store[k].start()
    for copy in store:
        copy.wait()


def shards(sizes, tokens, grad_output, query_gain, key_gain, short_query_gain, short_key_gain):
    nzh, ny, nx, nzl, nc = sizes
    nz, na = nzh * nzl, ny * nc
    width = tokens.shape[1]
    heads = width // HD
    span = na * SLOTS
    vmem = pl.BlockSpec(memory_space=pltpu.VMEM)
    hbm = pl.BlockSpec(memory_space=pl.ANY)
    dma = pltpu.SemaphoreType.DMA
    scratch = [
        pltpu.VMEM((2 * T, width), BF16),
        pltpu.VMEM((T + 16, width), BF16),
        pltpu.VMEM((16, width), BF16),
        pltpu.VMEM((heads, T, HD), BF16),
        pltpu.VMEM((heads, T, HD), BF16),
        pltpu.VMEM((heads, T, T), F32),
        pltpu.VMEM((heads, SLOTS, HD), F32),
        pltpu.VMEM((heads, SLOTS, HD), F32),
        pltpu.VMEM((heads, T, T), F32),
        pltpu.VMEM((heads, 2 * T, T), BF16),
        pltpu.VMEM((na, 16, HD), BF16),
        pltpu.VMEM((na, 16, HD), BF16),
        pltpu.VMEM((nx, 2, span, HD), BF16),
        pltpu.VMEM((nz, span, HD), BF16),
        pltpu.VMEM((nz, span, nx * span), F32),
        pltpu.VMEM((nz, span, nx * span), F32),
        pltpu.VMEM((nz, span, nx * span), BF16),
        pltpu.VMEM((nx, 4, nx * span), F32),
        pltpu.VMEM((nx, span, HD), BF16),
        pltpu.VMEM((nx, span, HD), BF16),
        pltpu.VMEM((nz, span, HD), BF16),
        pltpu.VMEM((nz, span, HD), BF16),
        pltpu.VMEM((na, SLOTS, HD), F32),
        pltpu.VMEM((na, SLOTS, HD), F32),
        pltpu.VMEM((na, SLOTS, HD), F32),
        pltpu.VMEM((heads, T, HD), BF16),
        pltpu.VMEM((heads, 2 * T, T), BF16),
        pltpu.VMEM((heads, 2 * T, HD), F32),
        pltpu.VMEM((heads, T, HD), BF16),
        pltpu.VMEM((heads, T, HD), BF16),
        pltpu.VMEM((heads, T, HD), F32),
        pltpu.VMEM((T, width), BF16),
        pltpu.VMEM((2, heads, HD), F32),
        pltpu.VMEM((heads, HD), F32),
        pltpu.VMEM((nx, heads, HD), BF16),
        pltpu.VMEM((ny, heads, HD), BF16),
        pltpu.VMEM((nz, heads, HD), BF16),
        pltpu.VMEM((2, heads, HD), F32),
        dma((3,)),
        dma((3,)),
        dma((3,)),
        dma((heads,)),
        dma((heads,)),
        dma((2, na)),
        dma((2, na)),
        dma((4, nx)),
        dma((4, nx)),
        dma((3, nz)),
        dma((3, nz)),
        dma((heads,)),
        dma((heads,)),
        dma((2,)),
        dma((2,)),
        dma((ny,)),
        dma((ny,)),
    ]
    first = pl.pallas_call(
        functools.partial(kernel, sizes),
        out_shape=(
            jax.ShapeDtypeStruct(tokens.shape, BF16),
            jax.ShapeDtypeStruct((4, width), F32),
        ),
        in_specs=[hbm, hbm, vmem, vmem, vmem, vmem],
        out_specs=(hbm, vmem),
        scratch_shapes=scratch,
        compiler_params=pltpu.CompilerParams(collective_id=0, has_side_effects=True),
        name="hourglass",
    )(
        tokens,
        grad_output,
        query_gain.reshape(1, width),
        key_gain.reshape(1, width),
        short_query_gain.reshape(1, width),
        short_key_gain.reshape(1, width),
    )
    return pl.pallas_call(
        relay,
        out_shape=(
            jax.ShapeDtypeStruct(tokens.shape, BF16),
            jax.ShapeDtypeStruct((4, width), F32),
        ),
        in_specs=[hbm, hbm],
        out_specs=(hbm, hbm),
        scratch_shapes=[pltpu.VMEM(tokens.shape, BF16), pltpu.VMEM((4, width), F32), dma((5,)), dma((5,))],
        name="relay",
    )(*first)


def build(mesh, sizes):
    finer = Mesh(mesh.devices.reshape(sizes), AXES)
    return jax.shard_map(
        functools.partial(shards, sizes),
        mesh=finer,
        in_specs=(P(AXES, None), P(AXES, None), P(), P(), P(), P()),
        out_specs=(P(AXES, None), P()),
        check_vma=False,
    )


def solution(mesh):
    return build(mesh, (2, 8, 4, 4, 2))
```

```python
import functools

import jax
import jax.numpy as jnp
from jax import lax
from jax.experimental import pallas as pl
from jax.experimental.pallas import tpu as pltpu
from jax.sharding import Mesh
from jax.sharding import PartitionSpec as P

AXES = ("zh", "y", "x", "zl", "c")
MESH = pl.DeviceIdType.MESH
T = 128
HD = 128
SLOTS = 8
NEGATIVE = -1e30
TEMPER = HD ** (-0.5)
F32 = jnp.float32
BF16 = jnp.bfloat16
GROUP = 8


def mm(a, b):
    return jnp.dot(a, b, preferred_element_type=F32)


def mm_nt(a, b):
    return lax.dot_general(a, b, (((1,), (1,)), ((), ())), preferred_element_type=F32)


def mm_tn(a, b):
    return lax.dot_general(a, b, (((0,), (0,)), ((), ())), preferred_element_type=F32)


def iota(shape, dim):
    return lax.broadcasted_iota(jnp.int32, shape, dim)


def remote(src, dst, send, recv, device):
    return pltpu.make_async_remote_copy(
        src_ref=src, dst_ref=dst, send_sem=send, recv_sem=recv, device_id=device, device_id_type=MESH
    )


def loop(count, body, start=0):
    def step(k, carry):
        body(k)
        return carry

    lax.fori_loop(start, count, step, 0)


def kernel(
    sizes,
    tok, gout, qg, kg, sqg, skg,
    out, gains,
    ctx, gsrc, tnext, qs, ks, own_scores, short, ext, wt, ws, pg_send, pg_recv, pgx, kz, prob, dprob, ds_short, stats,
    qgr_send, qgr_recv, kgr_send, kgr_recv, gp_send, gp_recv, gp_prev,
    gm, ds_local, gk_local, ret_send, ret_recv, acc, outv, gsum, gpart, gx, gy, gz, gfin,
    load_sem, next_send, next_recv, tok_send, tok_recv, a_send, a_recv, x_send, x_recv, z_send, z_recv,
    prev_send, prev_recv, d_send, d_recv, c_send, c_recv, y_send, y_recv,
):
    nzh, ny, nx, nzl, nc = sizes
    nz, na = nzh * nzl, ny * nc
    heads = na
    group = min(GROUP, heads)
    half = heads // 2
    stride = min(4, heads)
    span = na * SLOTS
    zh, y, x, zl, c = [lax.axis_index(name) for name in AXES]
    z = zh * nzl + zl
    a = y * nc + c
    chain = (((zh * ny + y) * nx + x) * nzl + zl) * nc + c
    total = nzh * ny * nx * nzl * nc

    def decode(index):
        return (
            index // (ny * nx * nzl * nc),
            index // (nx * nzl * nc) % ny,
            index // (nzl * nc) % nx,
            index // nc % nzl,
            index % nc,
        )

    following = decode((chain + 1) % total)
    previous = decode((chain + total - 1) % total)

    def at_a(other):
        return (zh, other // nc, x, zl, other % nc)

    def at_x(other):
        return (zh, y, other, zl, c)

    def at_z(other):
        return (other // nzl, y, x, other % nzl, c)

    barrier = pltpu.get_barrier_semaphore()
    drains = []

    def greet(device):
        pl.semaphore_signal(barrier, inc=1, device_id=device, device_id_type=MESH)

    greet(following)
    greet(previous)
    loop(na, lambda k: greet(at_a((a + k) % na)), 1)
    loop(nz, lambda k: greet(at_z((z + k) % nz)), 1)
    loop(nx, lambda k: greet(at_x((x + k) % nx)), 1)

    load_tok = pltpu.make_async_copy(tok, ctx.at[pl.ds(T, T)], load_sem.at[0])
    load_gout = pltpu.make_async_copy(gout, gsrc.at[pl.ds(0, T)], load_sem.at[1])
    load_tok.start()
    load_gout.start()

    pl.semaphore_wait(barrier, 2 + (na - 1) + (nz - 1) + (nx - 1))

    def columns(h):
        return pl.ds(pl.multiple_of(h * HD, HD), HD)

    head_tok = remote(tok.at[pl.ds(0, 16)], tnext, next_send.at[0], next_recv.at[0], previous)
    head_gout = remote(gout.at[pl.ds(0, 16)], gsrc.at[pl.ds(T, 16)], next_send.at[1], next_recv.at[1], previous)
    head_tok.start()
    head_gout.start()
    drains.append(head_tok.wait_send)
    drains.append(head_gout.wait_send)

    def tokens_of(h):
        return remote(
            tok.at[:, columns(h)], ctx.at[pl.ds(0, T), columns(h)], tok_send.at[h], tok_recv.at[h], following
        )

    loop(heads, lambda h: tokens_of(h).start())
    drains.append(lambda: loop(heads, lambda h: tokens_of(h).wait_send()))

    key_row = iota((T, T), 0)
    query_col = iota((T, T), 1)
    prior = key_row > query_col
    first_bias = jnp.where(chain == 0, NEGATIVE, 0.0)
    last_bias = jnp.where(chain == total - 1, NEGATIVE, 0.0)
    not_last = jnp.where(chain == total - 1, 0.0, 1.0)
    self_lane = iota((SLOTS, T), 1) == 0
    slot = iota((SLOTS, T), 0)
    row = iota((SLOTS, T), 1)
    keep = jnp.where(slot == SLOTS - 1, not_last, 1.0)
    pool = jnp.where((row > slot * 16) & (row <= slot * 16 + 16), keep, 0.0).astype(BF16)
    gpool = jnp.where((row >= slot * 16 + 16) & (row < slot * 16 + 32), 1.0, 0.0).astype(BF16)
    tail = iota((SLOTS, HD), 0) == SLOTS - 1

    load_tok.wait()
    load_gout.wait()

    def grouped(body):
        def several(g):
            for u in range(group):
                body(g * group + u)

        loop(heads // group, several)

    def prepare(h):
        cols = columns(h)
        own_f = ctx[pl.ds(T, T), cols].astype(F32)
        queries = (own_f * qg[:, cols]).astype(BF16)
        keys = (own_f * kg[:, cols]).astype(BF16)
        qs[h] = queries
        ks[h] = keys
        own_scores[h] = mm_nt(keys, queries) * TEMPER
        short[h] = mm(gpool, gsrc[pl.ds(0, T), cols])

    grouped(prepare)
    head_tok.wait_recv()
    head_gout.wait_recv()

    def extend(h):
        cols = columns(h)
        ext_f = tnext[:, cols].astype(F32)[:SLOTS]
        queries = (ext_f * qg[:, cols]).astype(BF16)
        keys = (ext_f * kg[:, cols]).astype(BF16)
        products = queries.astype(F32) * keys.astype(F32)
        same = jnp.broadcast_to(products.sum(axis=1, keepdims=True), (SLOTS, T))
        ext[h] = jnp.where(self_lane, same, mm_nt(queries, ks[h]) + last_bias) * TEMPER
        next_sum = gsrc[pl.ds(T, 16), cols].astype(F32).sum(axis=0, keepdims=True)
        short[h] += jnp.where(tail, next_sum, 0.0)

    def extend_values(h):
        cols = columns(h)
        ext_f = tnext[:, cols].astype(F32)[:SLOTS]
        weights = ext[h]
        found = mm(jnp.where(self_lane, 0.0, weights).astype(BF16), ctx[pl.ds(T, T), cols])
        found = found + weights[:, 0:1] * ext_f
        ext[h] = (ext_f + found).astype(BF16).astype(F32)

    grouped(extend)
    ext_weights = ext[...]
    ext_weights = jnp.exp(ext_weights - ext_weights.max(axis=2, keepdims=True))
    ext_weights = ext_weights * (1.0 / ext_weights.sum(axis=2, keepdims=True))
    ext[...] = ext_weights.astype(BF16).astype(F32)
    grouped(extend_values)

    def exchange(kind, h):
        send, recv, ssem, rsem = kind
        return remote(send.at[h], recv.at[a], ssem.at[h], rsem.at[a], at_a(h))

    def arrived(kind, h):
        send, recv, ssem, rsem = kind
        remote(send.at[h], recv.at[h], ssem.at[h], rsem.at[h], at_a(h)).wait_recv()

    def others_a(body):
        loop(na, lambda k: body((a + k) % na), 1)

    pg_kind = (pg_send, pg_recv, a_send.at[0], a_recv.at[0])
    gp_kind = (gp_send, gp_recv, a_send.at[1], a_recv.at[1])

    def forward(h):
        cols = columns(h)
        both = ctx[:, cols]
        both_f = both.astype(F32)
        keys = (both_f[:T] * kg[:, cols]).astype(BF16)
        scores = jnp.where(prior, mm_nt(keys, qs[h]) * TEMPER + first_bias, own_scores[h])
        weights = jnp.exp(scores - scores.max(axis=0, keepdims=True))
        weights = weights * (1.0 / weights.sum(axis=0, keepdims=True))
        wt[h] = weights
        split = jnp.concatenate([jnp.where(prior, weights, 0.0), jnp.where(prior, 0.0, weights)], axis=0).astype(BF16)
        ws[h] = split
        mixed = (both_f[T:] + mm_tn(split, both)).astype(BF16)
        pooled = mm(pool, mixed) + jnp.where(tail, ext[h][0:1], 0.0)
        pg_send[h] = jnp.concatenate([pooled * (1.0 / 16), short[h]], axis=0).astype(BF16)

    def dispatch(kind, h):
        @pl.when(h != a)
        def _():
            exchange(kind, h).start()

    def forward_group(g):
        for u in range(stride):
            tokens_of(g * stride + u).wait_recv()
        for u in range(stride):
            forward(g * stride + u)
        for u in range(stride):
            dispatch(pg_kind, g * stride + u)

    loop(heads // stride, forward_group)
    pg_recv[a] = pg_send[a]
    others_a(lambda h: arrived(pg_kind, h))
    drains.append(lambda: others_a(lambda h: exchange(pg_kind, h).wait_send()))

    blocks = pg_recv[...].astype(F32)
    pooled_own = blocks[:, :SLOTS].reshape(span, HD).astype(BF16)
    short_own = blocks[:, SLOTS:].reshape(span, HD)
    pgx[x, 0] = pooled_own
    pgx[x, 1] = short_own.astype(BF16)
    kz[z] = pooled_own

    def gather_x(other):
        return remote(pgx.at[x], pgx.at[x], x_send.at[0, other], x_recv.at[0, x], at_x(other))

    def gather_z(other):
        return remote(kz.at[z], kz.at[z], z_send.at[0, other], z_recv.at[0, z], at_z(other))

    def others_x(body):
        loop(nx, lambda k: body((x + k) % nx), 1)

    def others_z(body):
        loop(nz, lambda k: body((z + k) % nz), 1)

    def zig(k):
        half = (k + 1) // 2
        return (z + nz + half * (1 - 2 * ((k + 1) % 2))) % nz

    loop(nz - 1, lambda k: gather_z(zig(nz - 1 - k)).start())
    others_x(lambda o: gather_x(o).start())

    def x_arrived(phase, ref, other):
        remote(ref.at[other], ref.at[other], x_send.at[phase, other], x_recv.at[phase, other], at_x(other)).wait_recv()

    def z_arrived(phase, ref, other):
        remote(ref.at[other], ref.at[other], z_send.at[phase, other], z_recv.at[phase, other], at_z(other)).wait_recv()

    def position(zi, xi, index):
        source, place = index // SLOTS, index % SLOTS
        device = ((zi // nzl * ny + source // nc) * nx + xi) * nzl * nc + zi % nzl * nc + source % nc
        raw = device * SLOTS + place + 1
        return jnp.where(raw == total * SLOTS, 0, raw)

    head_cols = columns(a)
    gain_query = sqg[:, head_cols]
    gain_key = skg[:, head_cols]

    gain_both = gain_query * gain_key * TEMPER
    others_x(lambda o: x_arrived(0, pgx, o))
    wide = nx * span
    pooled_all = pgx[:, 0].reshape(wide, HD)
    short_all = pgx[:, 1].reshape(wide, HD)
    queries_all = (pooled_all.astype(F32) * gain_query).astype(BF16)
    query_index = iota((1, wide), 1)
    query_pos = position(z, query_index // span, query_index % span)
    key_index = iota((span, 1), 0)

    def first_pass(k, highest):
        b = zig(k)

        @pl.when(k > 0)
        def _():
            z_arrived(0, kz, b)

        values = kz[b]
        keys = (values.astype(F32) * gain_key).astype(BF16)
        visible = position(b, x, key_index) <= query_pos
        scores = jnp.where(visible, mm_nt(keys, queries_all) * TEMPER, NEGATIVE)
        prob[b] = scores
        dprob[b] = mm_nt(values, short_all)
        return jnp.maximum(highest, scores.max(axis=0, keepdims=True))

    highest = lax.fori_loop(0, nz, first_pass, jnp.full((1, wide), 0.1 * NEGATIVE, F32))
    drains.append(lambda: others_z(lambda o: gather_z(o).wait_send()))
    drains.append(lambda: others_x(lambda o: gather_x(o).wait_send()))

    def totals(k, carry):
        sums, dots = carry
        for b in (2 * k, 2 * k + 1):
            weights = jnp.exp(prob[b] - highest)
            prob[b] = weights
            sums = sums + weights.sum(axis=0, keepdims=True)
            dots = dots + (weights * dprob[b]).sum(axis=0, keepdims=True)
        return sums, dots

    zero = jnp.zeros((1, wide), F32)
    sums, dots = lax.fori_loop(0, nz // 2, totals, (zero, zero))
    stats[x] = jnp.concatenate([highest, sums, dots, jnp.zeros((1, wide), F32)], axis=0)

    def send_stats(other):
        return remote(stats.at[x], stats.at[x], x_send.at[1, other], x_recv.at[1, x], at_x(other))

    others_x(lambda o: send_stats(o).start())
    others_x(lambda o: x_arrived(1, stats, o))
    drains.append(lambda: others_x(lambda o: send_stats(o).wait_send()))

    def send_query(other):
        return remote(qgr_send.at[other], qgr_recv.at[x], x_send.at[2, other], x_recv.at[2, x], at_x(other))

    def send_key(other):
        return remote(kgr_send.at[other], kgr_recv.at[z], z_send.at[1, other], z_recv.at[1, z], at_z(other))

    pieces = [stats[s] for s in range(nx)]
    top = pieces[0][0:1]
    for piece in pieces[1:]:
        top = jnp.maximum(top, piece[0:1])
    all_sums = jnp.zeros((1, wide), F32)
    all_dots = jnp.zeros((1, wide), F32)
    for piece in pieces:
        factor = jnp.exp(piece[0:1] - top)
        all_sums = all_sums + piece[1:2] * factor
        all_dots = all_dots + piece[2:3] * factor
    inverse = 1.0 / all_sums
    mine = jnp.exp(highest - top) * inverse
    all_dots = all_dots * inverse

    def second_pass(k, gain_sum):
        for u in range(2):
            b = zig(nz - 1 - 2 * k - u)
            weights = prob[b] * mine
            ds = (weights * (dprob[b] - all_dots)).astype(BF16)
            ds_short[b] = ds
            grad_k = mm(ds, pooled_all)
            grad_v = mm(weights.astype(BF16), short_all)
            kgr_send[b] = (grad_k * gain_both + grad_v).astype(BF16)
            gain_sum = gain_sum + (grad_k * kz[b].astype(F32)).sum(axis=0, keepdims=True)
        send_key(zig(nz - 1 - 2 * k)).start()

        @pl.when(2 * k + 1 < nz - 1)
        def _():
            send_key(zig(nz - 2 - 2 * k)).start()

        return gain_sum

    gain_short = lax.fori_loop(0, nz // 2, second_pass, jnp.zeros((1, HD), F32))
    gsum[...] = jnp.zeros_like(gsum)
    gsum[a // half, pl.ds(half + a % half, 1), :] = gain_short
    grad_q = mm_tn(ds_short[...].reshape(nz * span, wide), kz[...].reshape(nz * span, HD)) * gain_both
    qgr_send[...] = grad_q.astype(BF16).reshape(nx, span, HD)
    others_x(lambda o: send_query(o).start())
    qgr_recv[x] = qgr_send[x]
    kgr_recv[z] = kgr_send[z]
    drains.append(lambda: others_x(lambda o: send_query(o).wait_send()))
    drains.append(lambda: others_z(lambda o: send_key(o).wait_send()))
    others_x(lambda o: x_arrived(2, qgr_recv, o))
    others_z(lambda o: z_arrived(1, kgr_recv, o))
    grad_pooled = short_own + qgr_recv[...].astype(F32).sum(axis=0) + kgr_recv[...].astype(F32).sum(axis=0)
    gp_send[...] = grad_pooled.reshape(na, SLOTS, HD)

    def beyond(h):
        after = (((zh * ny + h // nc) * nx + x) * nzl + zl) * nc + h % nc + 1
        return remote(gp_send.at[h], gp_prev.at[a], d_send.at[h], d_recv.at[a], decode(after % total))

    mine_next = jnp.where(c == 1, a - 1, heads)
    mine_own = jnp.where(c == 1, a, heads)

    def send_beyond(h):
        @pl.when(h != mine_next)
        def _():
            beyond(h).start()

    def drain_beyond(h):
        @pl.when(h != mine_next)
        def _():
            beyond(h).wait_send()

    def take_beyond(h):
        @pl.when(h != mine_own)
        def _():
            remote(gp_send.at[h], gp_prev.at[h], d_send.at[h], d_recv.at[h], previous).wait_recv()

    loop(heads, send_beyond)
    others_a(lambda h: exchange(gp_kind, h).start())
    gp_recv[a] = gp_send[a]

    @pl.when(c == 1)
    def _():
        gp_prev[a] = gp_send[jnp.maximum(a - 1, 0)]

    others_a(lambda h: arrived(gp_kind, h))
    loop(heads, take_beyond)
    drains.append(lambda: others_a(lambda h: exchange(gp_kind, h).wait_send()))
    drains.append(lambda: loop(heads, drain_beyond))

    token = iota((T, 16), 0)
    place = iota((T, 16), 1)
    source = jnp.where(token == 0, 15, (token + 15) // 16 - 1)
    spread = jnp.where(place == source, jnp.where(place == SLOTS - 1, not_last, 1.0) * (1.0 / 16), 0.0).astype(BF16)

    def give_back(h):
        return remote(ret_send.at[h], ret_recv.at[h], prev_send.at[h], prev_recv.at[h], previous)

    def scores_back(h):
        cols = columns(h)
        both = ctx[:, cols]
        rows = jnp.concatenate([gp_recv[h], gp_prev[h]], axis=0).astype(BF16)
        grad_mixed = gsrc[pl.ds(0, T), cols].astype(F32) + mm(spread, rows)
        acc[h] = grad_mixed
        incoming = grad_mixed.astype(BF16)
        gm[h] = incoming
        grads = mm_nt(both, incoming)
        grads = jnp.where(prior, grads[:T], grads[T:])
        weights = wt[h]
        dots = (weights * grads).sum(axis=0, keepdims=True)
        ds = weights * (grads - dots)
        ds = jnp.concatenate([jnp.where(prior, ds, 0.0), jnp.where(prior, 0.0, ds)], axis=0).astype(BF16)
        ds_local[h] = ds
        grad_k = mm(ds, both[T:])
        gk_local[h] = grad_k
        gain = (grad_k * both.astype(F32)).sum(axis=0, keepdims=True)
        gsum[h // half, pl.ds(h % half, 1), :] = gain

    partner = (zh, y, x, zl, 1 - c)

    def at_y(other):
        return (zh, other, x, zl, c)

    def others_y(body):
        loop(ny, lambda k: body((y + k) % ny), 1)

    halve = remote(gsum.at[1 - c], gpart, c_send.at[0], c_recv.at[0], partner)
    share = remote(gfin.at[c], gfin.at[c], c_send.at[1], c_recv.at[1], partner)

    def sum_z(other):
        return remote(gz.at[z], gz.at[z], z_send.at[2, other], z_recv.at[2, z], at_z(other))

    def sum_x(other):
        return remote(gx.at[x], gx.at[x], x_send.at[3, other], x_recv.at[3, x], at_x(other))

    def sum_y(other):
        return remote(gy.at[y], gy.at[y], y_send.at[other], y_recv.at[y], at_y(other))


    def values_back(h):
        cols = columns(h)
        gain = qg[:, cols] * kg[:, cols] * TEMPER
        to_keys = gk_local[h] * gain + mm(ws[h], gm[h])
        ret_send[h] = to_keys[:T].astype(BF16)
        acc[h] += mm_tn(ds_local[h], ctx[:, cols]) * gain + to_keys[T:]

    def values_group(g):
        for u in range(group):
            values_back(g * group + u)
        for u in range(group):
            give_back(g * group + u).start()

    grouped(scores_back)
    halve.start()
    values_group(0)
    halve.wait_recv()
    gy[y] = (gsum[c] + gpart[...]).astype(BF16)
    others_y(lambda o: sum_y(o).start())
    loop(heads // group, values_group, 1)
    drains.append(halve.wait_send)
    drains.append(lambda: loop(heads, lambda h: give_back(h).wait_send()))
    drains.append(lambda: others_y(lambda o: sum_y(o).wait_send()))

    others_y(lambda o: remote(gy.at[o], gy.at[o], y_send.at[o], y_recv.at[o], at_y(o)).wait_recv())
    gx[x] = gy[...].astype(F32).sum(axis=0).astype(BF16)
    others_x(lambda o: sum_x(o).start())
    others_x(lambda o: x_arrived(3, gx, o))
    drains.append(lambda: others_x(lambda o: sum_x(o).wait_send()))
    gz[z] = gx[...].astype(F32).sum(axis=0).astype(BF16)
    others_z(lambda o: sum_z(o).start())
    others_z(lambda o: z_arrived(2, gz, o))
    drains.append(lambda: others_z(lambda o: sum_z(o).wait_send()))
    gfin[c] = gz[...].astype(F32).sum(axis=0) * (TEMPER * float(total * T) ** (-0.5))
    share.start()
    drains.append(share.wait_send)

    def finish(h):
        give_back(h).wait_recv()
        outv[:, columns(h)] = (acc[h] + ret_recv[h].astype(F32)).astype(BF16)

    grouped(finish)
    store = pltpu.make_async_copy(outv, out, load_sem.at[2])
    store.start()
    drains.append(store.wait)
    remote(gfin.at[1 - c], gfin.at[1 - c], c_send.at[1], c_recv.at[1], partner).wait_recv()
    for side in range(2):
        rows = gfin[side]
        for r in range(half):
            cols = pl.ds((side * half + r) * HD, HD)
            local, pooled = rows[r : r + 1], rows[half + r : half + r + 1]
            gains[:, cols] = jnp.concatenate(
                [local * kg[:, cols], local * qg[:, cols], pooled * skg[:, cols], pooled * sqg[:, cols]], axis=0
            )

    for wait in drains:
        wait()


def relay(first, second, out, gains, hold, small, arrive, leave):
    rows = hold.shape[0] // 4
    pairs = [(first.at[pl.ds(k * rows, rows)], hold.at[pl.ds(k * rows, rows)], out.at[pl.ds(k * rows, rows)]) for k in range(4)]
    pairs.append((second, small, gains))
    fetch = [pltpu.make_async_copy(i, m, arrive.at[k]) for k, (i, m, o) in enumerate(pairs)]
    store = [pltpu.make_async_copy(m, o, leave.at[k]) for k, (i, m, o) in enumerate(pairs)]
    for copy in fetch:
        copy.start()
    for k in range(5):
        fetch[k].wait()
        store[k].start()
    for copy in store:
        copy.wait()


def shards(sizes, tokens, grad_output, query_gain, key_gain, short_query_gain, short_key_gain):
    nzh, ny, nx, nzl, nc = sizes
    nz, na = nzh * nzl, ny * nc
    width = tokens.shape[1]
    heads = width // HD
    span = na * SLOTS
    vmem = pl.BlockSpec(memory_space=pltpu.VMEM)
    hbm = pl.BlockSpec(memory_space=pl.ANY)
    dma = pltpu.SemaphoreType.DMA
    scratch = [
        pltpu.VMEM((2 * T, width), BF16),
        pltpu.VMEM((T + 16, width), BF16),
        pltpu.VMEM((16, width), BF16),
        pltpu.VMEM((heads, T, HD), BF16),
        pltpu.VMEM((heads, T, HD), BF16),
        pltpu.VMEM((heads, T, T), F32),
        pltpu.VMEM((heads, SLOTS, HD), F32),
        pltpu.VMEM((heads, SLOTS, HD), F32),
        pltpu.VMEM((heads, T, T), F32),
        pltpu.VMEM((heads, 2 * T, T), BF16),
        pltpu.VMEM((na, 16, HD), BF16),
        pltpu.VMEM((na, 16, HD), BF16),
        pltpu.VMEM((nx, 2, span, HD), BF16),
        pltpu.VMEM((nz, span, HD), BF16),
        pltpu.VMEM((nz, span, nx * span), F32),
        pltpu.VMEM((nz, span, nx * span), F32),
        pltpu.VMEM((nz, span, nx * span), BF16),
        pltpu.VMEM((nx, 4, nx * span), F32),
        pltpu.VMEM((nx, span, HD), BF16),
        pltpu.VMEM((nx, span, HD), BF16),
        pltpu.VMEM((nz, span, HD), BF16),
        pltpu.VMEM((nz, span, HD), BF16),
        pltpu.VMEM((na, SLOTS, HD), F32),
        pltpu.VMEM((na, SLOTS, HD), F32),
        pltpu.VMEM((na, SLOTS, HD), F32),
        pltpu.VMEM((heads, T, HD), BF16),
        pltpu.VMEM((heads, 2 * T, T), BF16),
        pltpu.VMEM((heads, 2 * T, HD), F32),
        pltpu.VMEM((heads, T, HD), BF16),
        pltpu.VMEM((heads, T, HD), BF16),
        pltpu.VMEM((heads, T, HD), F32),
        pltpu.VMEM((T, width), BF16),
        pltpu.VMEM((2, heads, HD), F32),
        pltpu.VMEM((heads, HD), F32),
        pltpu.VMEM((nx, heads, HD), BF16),
        pltpu.VMEM((ny, heads, HD), BF16),
        pltpu.VMEM((nz, heads, HD), BF16),
        pltpu.VMEM((2, heads, HD), F32),
        dma((3,)),
        dma((3,)),
        dma((3,)),
        dma((heads,)),
        dma((heads,)),
        dma((2, na)),
        dma((2, na)),
        dma((4, nx)),
        dma((4, nx)),
        dma((3, nz)),
        dma((3, nz)),
        dma((heads,)),
        dma((heads,)),
        dma((heads,)),
        dma((heads,)),
        dma((2,)),
        dma((2,)),
        dma((ny,)),
        dma((ny,)),
    ]
    first = pl.pallas_call(
        functools.partial(kernel, sizes),
        out_shape=(
            jax.ShapeDtypeStruct(tokens.shape, BF16),
            jax.ShapeDtypeStruct((4, width), F32),
        ),
        in_specs=[hbm, hbm, vmem, vmem, vmem, vmem],
        out_specs=(hbm, vmem),
        scratch_shapes=scratch,
        compiler_params=pltpu.CompilerParams(collective_id=0, has_side_effects=True),
        name="hourglass",
    )(
        tokens,
        grad_output,
        query_gain.reshape(1, width),
        key_gain.reshape(1, width),
        short_query_gain.reshape(1, width),
        short_key_gain.reshape(1, width),
    )
    return pl.pallas_call(
        relay,
        out_shape=(
            jax.ShapeDtypeStruct(tokens.shape, BF16),
            jax.ShapeDtypeStruct((4, width), F32),
        ),
        in_specs=[hbm, hbm],
        out_specs=(hbm, hbm),
        scratch_shapes=[pltpu.VMEM(tokens.shape, BF16), pltpu.VMEM((4, width), F32), dma((5,)), dma((5,))],
        name="relay",
    )(*first)


def build(mesh, sizes):
    finer = Mesh(mesh.devices.reshape(sizes), AXES)
    return jax.shard_map(
        functools.partial(shards, sizes),
        mesh=finer,
        in_specs=(P(AXES, None), P(AXES, None), P(), P(), P(), P()),
        out_specs=(P(AXES, None), P()),
        check_vma=False,
    )


def solution(mesh):
    return build(mesh, (2, 8, 4, 4, 2))
```
